256 devices in a mesh: section: 4 (over x_hi, core), feat: 64 (over y, x_lo, z).
Axes of the slice: x: 4 (x_hi: 2, x_lo: 2; x = x_hi * 2 + x_lo), y: 4, z: 8, core: 2. Of those that a mesh axis runs over, the one named last changes fastest.
Arguments:
- residual: bfloat16 [4, 128, 4096], P('section'), may hold values from -6 to 6
- enc_weight: bfloat16 [4, 4096, 16384], P('section', None, 'feat'), may hold values from -0.09375 to 0.09375
- dec_weight: bfloat16 [4, 16384, 4, 4096], P('section', 'feat'), may hold values from -2 to 2
- latent_ids: int32 [4, 128, 64], P('section'), may hold values from 0 to 16383, all different within a row
Outputs:
- written: bfloat16 [4, 4096, 128], P('section', 'feat')
The draws below stay inside these ranges and needn't reach their ends.
Inputs may be any that keep to these rules, and one draw needn't show every extreme that they name: Each row latent_ids[l, n, :] names 64 different latents.
All inputs are finite; a program needn't handle non-finite values.
Results may differ from the reference program's by a relative error of at most 0.0049.
Values may be sent and summed in bfloat16 or wider, within the bound.
A program may use at most 128 MiB of HBM per device.

```python
import jax
import jax.numpy as jnp
from jax import lax

D = 4096
F = 16384
K = 64
TOK = 128
L = 4


def spiked(values, own_key, source, target, parts, factor):
    owner, partner = [(jnp.arange(values.shape[position]) // (values.shape[position] // parts)).reshape([-1 if axis == position else 1 for axis in range(values.ndim)]) for position in (source, target)]
    chosen = jax.random.permutation(own_key, parts)[partner]
    strong = (owner == chosen) | (owner == (partner + parts // 2) % parts)
    return jnp.where(strong, factor * values, values)


def shard_levels(stream_key, dims, cuts, low, high):
    def one(dim, shards_of):
        heights = jax.random.uniform(jax.random.fold_in(jax.random.fold_in(stream_key, 6), dim), (shards_of,), jnp.float32, low / len(cuts), high / len(cuts))
        return jnp.repeat(jnp.exp(heights), dims[dim] // shards_of).reshape((-1,) + (1,) * (len(dims) - dim - 1))

    gain = one(*cuts[0])
    for cut in cuts[1:]:
        gain = gain * one(*cut)
    return gain


def different_ones(rng, rows, count, top, lift):
    ranking = jax.random.permutation(jax.random.fold_in(rng, 1), count)
    favour = ranking
    for power in range(3):
        favour = favour * favour // count
    favour = favour * lift // count
    lots = jax.random.randint(jax.random.fold_in(rng, 2), (rows, count), 0, 4096) + favour
    holders = jax.random.permutation(jax.random.fold_in(rng, 3), rows)[jnp.arange(count) % rows]
    lots = jnp.where(jnp.arange(rows)[:, None] == holders[None, :], 1 << 14, lots)
    merit = lots * count + jnp.arange(count)
    return lax.top_k(merit.astype(jnp.int32), top)[1].astype(jnp.int32)


def bell_draw(rng, extent, width, most, split=(), held_as=jnp.bfloat16):
    factor_of = shard_levels(rng, extent, split, -0.22, 0.18) if split else 1.0
    drawn = jax.random.normal(rng, extent, jnp.float32) * width * factor_of
    return jnp.minimum(jnp.maximum(drawn, -most), most).astype(held_as)


def heavy_noise(rng, extent, scale, reach, pieces, heavy, dtype=jnp.bfloat16):
    array = scale * jax.random.normal(rng, extent, jnp.float32)
    if pieces:
        array = array * shard_levels(rng, extent, pieces, -0.22, 0.18)
    return jnp.clip(spiked(array, jax.random.fold_in(rng, 3), *heavy), -reach, reach).astype(dtype)


def setup_inputs(seed: int = 0) -> dict:
    key_of = jax.random.split(jax.random.key(seed), 5)
    residual = bell_draw(key_of[0], (L, TOK, D), 1.0, 6.0, ((0, 4),))
    enc_weight = bell_draw(key_of[1], (L, D, F), D ** -0.5, 0.09375, ((0, 4), (2, 64)))
    dec_weight = heavy_noise(key_of[2], (L, F, L, D), K ** -0.5, 2.0, ((0, 4), (1, 64)), (1, 3, 64, 4.0))
    latent_ids = different_ones(key_of[3], L * TOK, F, K, 32).reshape((L, TOK, K))
    return {"residual": residual, "enc_weight": enc_weight, "dec_weight": dec_weight, "latent_ids": latent_ids}


def reference(residual, enc_weight, dec_weight, latent_ids):
    layers = residual.shape[0]
    totals = [jnp.zeros((TOK, D), jnp.float32) for target in range(layers)]
    for source in range(layers):
        ids_here = latent_ids[source]
        enc_cols = jnp.take(enc_weight[source], ids_here, axis=1)
        pre_acts = jnp.einsum("nd,dnk->nk", residual[source].astype(jnp.float32), enc_cols.astype(jnp.float32))
        latent_vals = jnp.maximum(pre_acts, 0.0).astype(jnp.bfloat16)
        for target in range(source, layers):
            dec_rows = jnp.take(dec_weight[source, :, target, :], ids_here, axis=0)
            contrib = jnp.einsum("nk,nkd->nd", latent_vals.astype(jnp.float32), dec_rows.astype(jnp.float32))
            totals[target] = totals[target] + contrib
    return jnp.stack([block.T for block in totals]).astype(jnp.bfloat16)
```

```python
import jax
import jax.numpy as jnp
from jax import lax
from jax.experimental import pallas as pl
from jax.experimental.pallas import tpu as pltpu
from jax.sharding import PartitionSpec as P

MESH = pl.DeviceIdType.MESH
F32, BF16 = jnp.float32, jnp.bfloat16
TOK = 128
LANES = 512
A0, A1, B0, B1 = (0, 32), (32, 32), (64, 32), (96, 32)
B = (64, 64)
ORDER = (2, 1, 3, 0)
NEAR, FAR = 0, 1


def when(cond, run):
    if cond is None:
        run()
    else:
        pl.when(cond)(run)


def kernel(res_hbm, enc_hbm, dec_hbm, ids_hbm, out_ref, res, enc, ids, dec, lhs, acc, core_out, core_in, sent, got,
           z_sum, z_out, z_in, load_sem, send_sem, recv_sem):
    section, feat = lax.axis_index("section"), lax.axis_index("feat")
    core, xh = section % 2, section // 2
    y, xl, z = feat // 16, (feat // 8) % 2, feat % 8
    flip = {0: y, 1: y + 1 - 2 * (y % 2), 2: (y + 2) % 4, 3: 3 - y}

    def device(core_=core, xh_=xh, y_=y, xl_=xl, z_=z):
        return (xh_ * 2 + core_, (y_ * 2 + xl_) * 8 + z_)

    other_core = device(core_=1 - core)
    y_by = {1: device(y_=flip[1]), 3: device(y_=flip[3])}
    x_side = device(xl_=1 - xl)
    x_cross = device(xh_=1 - xh, xl_=1 - xl)
    z_by = {k: device(z_=(z + k) % 8) for k in range(1, 8)}

    barrier = pltpu.get_barrier_semaphore()
    for peer in [other_core, y_by[1], y_by[3], x_side, x_cross] + list(z_by.values()):
        pl.semaphore_signal(barrier, inc=1, device_id=peer, device_id_type=MESH)

    loads = {}

    def load(key, src, dst):
        loads[key] = pltpu.make_async_copy(src, dst, load_sem.at[len(loads)])
        loads[key].start()

    load("ids", ids_hbm.at[0], ids)
    load("res", res_hbm.at[0], res)
    load("enc", enc_hbm.at[0], enc)
    for m in ORDER:
        for r in range(2):
            half = xl if r == 0 else 1 - xl
            for j in range(4):
                load((m, r, j), dec_hbm.at[:, flip[m] * 8 + half * 4 + j], dec.at[m, r, j])

    loads["ids"].wait()
    local_ids = ids[...] - feat * 256
    latent = lax.broadcasted_iota(jnp.int32, (256, TOK), 0)
    active = latent == local_ids[0:1, :]
    for k in range(1, 64):
        active = active | (latent == local_ids[k:k + 1, :])
    active = jnp.where(active, 1.0, 0.0).astype(F32).T
    spread = (lax.broadcasted_iota(jnp.int32, (256, 1024), 1) // 4 == lax.broadcasted_iota(jnp.int32, (256, 1024), 0))
    spread = jnp.where(spread, 1.0, 0.0).astype(BF16)
    loads["res"].wait()
    loads["enc"].wait()
    pre_acts = jnp.dot(res[...], enc[...], preferred_element_type=F32)
    acts = (jnp.maximum(pre_acts, 0.0) * active).astype(BF16)
    acts = jnp.dot(acts, spread, preferred_element_type=F32).astype(BF16)
    place = lax.broadcasted_iota(jnp.int32, (TOK, 1024), 1) % 4
    for row, target in enumerate((1 - core, 3 - core, core, core + 2)):
        lhs[pl.ds(row * TOK, TOK), :] = jnp.where((place == target) & (target >= section), acts, jnp.zeros_like(acts))

    numbers = {}

    def number(key):
        return numbers.setdefault(key, len(numbers))

    pending = []

    def remote(key, src, dst, peer):
        i = number(key)
        return pltpu.make_async_remote_copy(
            src_ref=src, dst_ref=dst, send_sem=send_sem.at[i], recv_sem=recv_sem.at[i], device_id=peer, device_id_type=MESH
        )

    def start(cond, key, src, dst, peer):
        when(cond, lambda: remote(key, src, dst, peer).start())
        pending.append((cond, key, src, dst, peer))

    def arrived(key, src, dst):
        remote(key, src, dst, other_core).wait_recv()

    near_here, far_here = xh == 0, xh == 1

    def rows(piece):
        return pl.ds(piece[0], piece[1])

    def pack(t, m, r, piece):
        sent[t, m, r, rows(piece), :] = acc[t, m, r, rows(piece), :].astype(BF16)

    def take(key, step, t, m, r, piece):
        region = got.at[step, t, m, r, rows(piece), :]
        arrived(key, sent.at[t, m, r, rows(piece), :], region)
        acc[t, m, r, rows(piece), :] += got[step, t, m, r, rows(piece), :].astype(F32)

    def send(cond, key, step, t, m, r, piece, to_m, to_r, peer):
        start(cond, key, sent.at[t, m, r, rows(piece), :], got.at[step, t, to_m, to_r, rows(piece), :], peer)

    BOTH = pl.ds(0, 2)
    Y_PATH = {A0: (1, 3), A1: (3, 1), B0: (1, 3), B1: (3, 1)}

    def y_first(step, t, m, r, piece, name):
        k = Y_PATH[piece][0]
        pack(t, m, r, piece)
        send(None, (name, "y1", piece, m ^ k), step, t, m, r, piece, m ^ k, r, y_by[k])

    def y_second(step, t, r, piece, name):
        k = Y_PATH[piece][1]
        pack(t, k, r, piece)
        send(None, (name, "y2", piece), step, t, k, r, piece, 0, r, y_by[k])

    def multiply(m):
        for r in range(2):
            for j in range(4):
                loads[(m, r, j)].wait()
            for n in range(2):
                w = jnp.concatenate([dec.at[m, r, 2 * n + i].reshape(1024, 128)[...] for i in range(2)], axis=1)
                out = jnp.dot(lhs[...], w, preferred_element_type=F32)
                lanes = pl.ds(n * 256, 256)
                for t in range(2):
                    core_out[t, m, r, :, lanes] = out[t * TOK:(t + 1) * TOK].astype(BF16)
                    acc[t, m, r, :, lanes] = out[(2 + t) * TOK:(3 + t) * TOK]
        for t in (FAR, NEAR):
            start(section == 0 if t == NEAR else section != 3, ("core", t, m), core_out.at[t, m], core_in.at[t, m], other_core)

    def collect(m):
        for t in (FAR, NEAR):
            @pl.when(section == 1 if t == NEAR else section != 2)
            def _():
                arrived(("core", t, m), core_out.at[t, m], core_in.at[t, m])
                acc[t, m] += core_in[t, m].astype(F32)

    def spread_out(m):
        def side(t):
            for piece in (A0, A1):
                if m in (2, Y_PATH[piece][0]):
                    k = Y_PATH[piece][0]
                    pack(t, m, BOTH, piece)
                    send(near_here if t == NEAR else None, ("a", t, "y1", piece, m ^ k), 0, t, m, BOTH, piece, m ^ k, BOTH, y_by[k])

        pack(FAR, m, BOTH, B)
        side(FAR)
        send(None, ("b", "side", m), 0, FAR, m, xh, B0, m, 1 - xh, x_side)
        for r in range(2):
            send(near_here, ("b", "cross", m, 1 - r), 0, FAR, m, r, B1, m, 1 - r, x_cross)

        pack(NEAR, m, 1, B)
        side(NEAR)
        send(near_here, ("b", "near", m), 0, NEAR, m, 1, B, m, 0, x_side)

    pl.semaphore_wait(barrier, 12)
    before = None
    for m in ORDER:
        multiply(m)
        if before is not None:
            collect(before)
            spread_out(before)
        before = m
    collect(before)
    spread_out(before)

    def a_first(t, cond):
        for piece in (A0, A1):
            k1, k2 = Y_PATH[piece]

            def add(m):
                take(("a", t, "y1", piece, m), 0, t, m, BOTH, piece)

            def both():
                add(k2)
                pack(t, k2, BOTH, piece)

            when(cond, both)
            send(cond, ("a", t, "y2", piece), 1, t, k2, BOTH, piece, 0, BOTH, y_by[k2])
            when(cond, lambda: add(0))

    a_first(FAR, None)
    a_first(NEAR, near_here)

    for m in ORDER:
        take(("b", "side", m), 0, FAR, m, 1 - xh, B0)

        @pl.when(far_here)
        def _():
            for r in range(2):
                take(("b", "cross", m, r), 0, FAR, m, r, B1)

        when(near_here, lambda: pack(FAR, m, 1, B0))
        when(far_here, lambda: pack(FAR, m, 1, B1))
        send(near_here, ("b", "cross2", m), 1, FAR, m, 1, B0, m, 0, x_cross)
        send(far_here, ("b", "side2", m), 1, FAR, m, 1, B1, m, 0, x_side)

        @pl.when(near_here)
        def _():
            take(("b", "near", m), 0, NEAR, m, 0, B)

    def a_second(t, cond):
        for piece in (A0, A1):
            when(cond, lambda: take(("a", t, "y2", piece), 1, t, 0, BOTH, piece))

    a_second(FAR, None)
    pack(FAR, 0, BOTH, (0, 64))
    send(None, ("a", "side"), 2, FAR, 0, xh, A0, 0, 1 - xh, x_side)
    for r in range(2):
        send(near_here, ("a", "cross", 1 - r), 2, FAR, 0, r, A1, 0, 1 - r, x_cross)
    a_second(NEAR, near_here)
    pack(NEAR, 0, 1, (0, 64))
    send(near_here, ("a", "near"), 2, NEAR, 0, 1, (0, 64), 0, 0, x_side)

    for m in ORDER:
        @pl.when(far_here)
        def _():
            take(("b", "cross2", m), 1, FAR, m, 0, B0)
            take(("b", "side2", m), 1, FAR, m, 0, B1)

        for piece in (B0, B1):
            if m in (2, Y_PATH[piece][0]):
                y_first(2, xh, m, 0, piece, "b")

    take(("a", "side"), 2, FAR, 0, 1 - xh, A0)

    @pl.when(far_here)
    def _():
        for r in range(2):
            take(("a", "cross", r), 2, FAR, 0, r, A1)

    when(near_here, lambda: pack(FAR, 0, 1, A0))
    when(far_here, lambda: pack(FAR, 0, 1, A1))
    send(near_here, ("a", "cross2"), 3, FAR, 0, 1, A0, 0, 0, x_cross)
    send(far_here, ("a", "side2"), 3, FAR, 0, 1, A1, 0, 0, x_side)

    for piece in (B0, B1):
        k1, k2 = Y_PATH[piece]
        take(("b", "y1", piece, k2), 2, xh, k2, 0, piece)
        y_second(3, xh, 0, piece, "b")
        take(("b", "y1", piece, 0), 2, xh, 0, 0, piece)

    @pl.when(near_here)
    def _():
        take(("a", "near"), 2, NEAR, 0, 0, (0, 64))

    @pl.when(far_here)
    def _():
        take(("a", "cross2"), 3, FAR, 0, 0, A0)
        take(("a", "side2"), 3, FAR, 0, 0, A1)

    for piece in (B0, B1):
        take(("b", "y2", piece), 3, xh, 0, 0, piece)

    turned = acc[xh, 0, 0].T.reshape(8, 64, TOK)
    z_sum[...] = turned
    z_out[...] = turned.astype(BF16)
    for k in (4, 3, 5, 2, 6, 1, 7):
        start(None, ("z", k), z_out.at[(z + k) % 8], z_in.at[k], z_by[k])
    total = z_sum[z]
    for k in (1, 7, 2, 6, 3, 5, 4):
        arrived(("z", k), z_out.at[0], z_in.at[k])
        total = total + z_in[k].astype(F32)
    out_ref[0] = total.astype(BF16)

    for cond, key, src, dst, peer in pending:
        when(cond, lambda: remote(key, src, dst, peer).wait_send())


def local(residual, enc_weight, dec_weight, latent_ids):
    dec = dec_weight[0].reshape(256, 4, 32, 128).transpose(0, 2, 1, 3)
    ids = latent_ids.transpose(0, 2, 1)
    blocks = (2, 4, 2, TOK, LANES)
    return pl.pallas_call(
        kernel,
        out_shape=jax.ShapeDtypeStruct((1, 64, TOK), BF16),
        in_specs=[pl.BlockSpec(memory_space=pl.ANY)] * 4,
        out_specs=pl.BlockSpec(memory_space=pltpu.VMEM),
        scratch_shapes=[
            pltpu.VMEM((TOK, 4096), BF16),
            pltpu.VMEM((4096, 256), BF16),
            pltpu.VMEM((64, TOK), jnp.int32),
            pltpu.VMEM((4, 2, 4, 256, 4, 128), BF16),
            pltpu.VMEM((4 * TOK, 1024), BF16),
            pltpu.VMEM(blocks, F32),
            pltpu.VMEM(blocks, BF16),
            pltpu.VMEM(blocks, BF16),
            pltpu.VMEM(blocks, BF16),
            pltpu.VMEM((4,) + blocks, BF16),
            pltpu.VMEM((8, 64, TOK), F32),
            pltpu.VMEM((8, 64, TOK), BF16),
            pltpu.VMEM((8, 64, TOK), BF16),
            pltpu.SemaphoreType.DMA((40,)),
            pltpu.SemaphoreType.DMA((96,)),
            pltpu.SemaphoreType.DMA((96,)),
        ],
        compiler_params=pltpu.CompilerParams(
            collective_id=0, has_side_effects=True, vmem_limit_bytes=60 * 1024 * 1024
        ),
    )(residual, enc_weight, dec, ids)


def solution(mesh):
    in_specs = (
        P("section", None, None),
        P("section", None, "feat"),
        P("section", "feat", None, None),
        P("section", None, None),
    )
    return jax.shard_map(local, mesh=mesh, in_specs=in_specs, out_specs=P("section", "feat", None), check_vma=False)
```

```python
import jax
import jax.numpy as jnp
from jax import lax
from jax.experimental import pallas as pl
from jax.experimental.pallas import tpu as pltpu
from jax.sharding import PartitionSpec as P

MESH = pl.DeviceIdType.MESH
F32, BF16 = jnp.float32, jnp.bfloat16
TOK = 128
A0, A1, B0, B1 = (0, 32), (32, 32), (64, 32), (96, 32)
A, B = (0, 64), (64, 64)
NEAR, FAR = 0, 1
TILES = (2, 1, 3, 0)
Y_PATH = {A0: (1, 3), A1: (3, 1), B0: (1, 3), B1: (3, 1)}


def when(cond, run):
    if cond is None:
        run()
    else:
        @pl.when(cond)
        def _():
            run()


def rows(piece):
    return pl.ds(piece[0], piece[1])


def kernel(res_hbm, enc_hbm, dec_hbm, ids_hbm, out_ref, res, enc, ids, dec, lhs, acc, core_out, core_in, sent, got,
           z_own, z_out, z_in, load_sem, send_sem, recv_sem):
    section, feat = lax.axis_index("section"), lax.axis_index("feat")
    core, xh = section % 2, section // 2
    y, xl, z = feat // 16, (feat // 8) % 2, feat % 8
    z_pair, z_low = z // 2, z % 2
    flip = {0: y, 1: y + 1 - 2 * (y % 2), 2: (y + 2) % 4, 3: 3 - y}
    near_here, far_here = xh == 0, xh == 1

    def device(core_=core, xh_=xh, y_=y, xl_=xl, z_=z):
        return (xh_ * 2 + core_, (y_ * 2 + xl_) * 8 + z_)

    other_core = device(core_=1 - core)
    y_by = {1: device(y_=flip[1]), 3: device(y_=flip[3])}
    x_side = device(xl_=1 - xl)
    x_cross = device(xh_=1 - xh, xl_=1 - xl)
    tile_of = {p: (z_pair + p) % 4 for p in TILES}
    z_by = {(p, e): device(z_=2 * tile_of[p] + (z_low if e == 0 else 1 - z_low)) for p in TILES for e in range(2)}
    z_by.pop((0, 0))

    barrier = pltpu.get_barrier_semaphore()
    for peer in [other_core, y_by[1], y_by[3], x_side, x_cross] + list(z_by.values()):
        pl.semaphore_signal(barrier, inc=1, device_id=peer, device_id_type=MESH)

    loads = {}

    def load(key, src, dst):
        copy = pltpu.make_async_copy(src, dst, load_sem.at[len(loads)])
        loads[key] = copy
        return copy

    def load_dec(p, t):
        for m in range(4):
            for r in range(2):
                tile = flip[m] * 8 + (xl if r == 0 else 1 - xl) * 4 + tile_of[p]
                load((p, t, m, r), dec_hbm.at[:, tile, t], dec.at[p, t, m, r])
        when(near_here if t == NEAR else None, lambda: [loads[(p, t, m, r)].start() for m in range(4) for r in range(2)])

    load("ids", ids_hbm.at[0], ids).start()
    load("res", res_hbm.at[0], res).start()
    load("enc", enc_hbm.at[0], enc).start()
    for p in TILES:
        load_dec(p, FAR)
        load_dec(p, NEAR)

    for nothing_comes, t in ((section == 0, NEAR), (section == 2, FAR)):
        @pl.when(nothing_comes)
        def _():
            for p in TILES:
                core_in[p, t] = jnp.zeros((4, 2, TOK, 128), BF16)

    loads["ids"].wait()
    local_ids = ids[...] - feat * 256
    latent = lax.broadcasted_iota(jnp.int32, (256, TOK), 0)
    active = latent == local_ids[0:1, :]
    for k in range(1, 64):
        active = active | (latent == local_ids[k:k + 1, :])
    active = jnp.where(active, 1.0, 0.0).astype(F32).T
    spread = (lax.broadcasted_iota(jnp.int32, (256, 512), 1) // 2 == lax.broadcasted_iota(jnp.int32, (256, 512), 0))
    spread = jnp.where(spread, 1.0, 0.0).astype(BF16)
    loads["res"].wait()
    loads["enc"].wait()
    pre_acts = jnp.dot(res[...], enc[...], preferred_element_type=F32)
    acts = (jnp.maximum(pre_acts, 0.0) * active).astype(BF16)
    acts = jnp.dot(acts, spread, preferred_element_type=F32).astype(BF16)
    place = lax.broadcasted_iota(jnp.int32, (TOK, 512), 1) % 2
    for t in range(2):
        for row, low in enumerate((1 - core, core)):
            keep = (place == low) & (2 * t + low >= section)
            lhs[t, pl.ds(row * TOK, TOK), :] = jnp.where(keep, acts, jnp.zeros_like(acts))

    numbers = {}
    pending = []

    def remote(key, src, dst, peer):
        i = numbers.setdefault(key, len(numbers))
        return pltpu.make_async_remote_copy(
            src_ref=src, dst_ref=dst, send_sem=send_sem.at[i], recv_sem=recv_sem.at[i], device_id=peer, device_id_type=MESH
        )

    def send(cond, key, src, dst, peer):
        when(cond, lambda: remote(key, src, dst, peer).start())
        pending.append((cond, key, src, dst, peer))

    def arrived(key, region):
        remote(key, region, region, other_core).wait_recv()

    ALL, BOTH = pl.ds(0, 4), pl.ds(0, 2)

    def out(p, t, m, r, piece):
        return sent.at[p, t, m, r, rows(piece), :]

    def slot(step, p, t, m, r, piece):
        return got.at[step, p, t, m, r, rows(piece), :]

    def have(p, t, m, r, piece):
        return acc[p, t, m, r, rows(piece), :]

    def came(step, p, t, m, r, piece):
        return got[step, p, t, m, r, rows(piece), :].astype(F32)

    def keep(p, t, m, r, piece, value):
        acc[p, t, m, r, rows(piece), :] = value

    def pack(p, t, m, r, piece, value):
        sent[p, t, m, r, rows(piece), :] = value.astype(BF16)

    def multiply(p):
        def one(t):
            for m in range(4):
                for r in range(2):
                    loads[(p, t, m, r)].wait()
                w = jnp.concatenate([dec.at[p, t, m, r].reshape(512, 128)[...] for r in range(2)], axis=1)
                both = jnp.dot(lhs[t], w, preferred_element_type=F32)
                for r in range(2):
                    core_out[p, t, m, r] = both[0:TOK, r * 128:(r + 1) * 128].astype(BF16)
                    acc[p, t, m, r] = both[TOK:2 * TOK, r * 128:(r + 1) * 128]

        one(FAR)
        send(section != 3, (p, "core", FAR), core_out.at[p, FAR], core_in.at[p, FAR], other_core)
        when(near_here, lambda: one(NEAR))
        send(section == 0, (p, "core", NEAR), core_out.at[p, NEAR], core_in.at[p, NEAR], other_core)

    FIRST = {A0: 1, A1: 2, B0: 1, B1: 2}
    SLOT_OF = {A0: (0, 3), A1: (1, 0), B0: (0, 3), B1: (1, 0)}

    def y_one(cond, key, step, p, t, r, piece):
        send(cond, key, sent.at[p, t, pl.ds(FIRST[piece], 2), r, rows(piece), :],
             got.at[step, p, t, BOTH, r, rows(piece), :], y_by[Y_PATH[piece][0]])

    def y_two(cond, key, step, p, t, r, piece):
        k = Y_PATH[piece][1]
        send(cond, key, out(p, t, k, r, piece), slot(step, p, t, 0, r, piece), y_by[k])

    def first(p):
        def core_sum(t, m, r, piece):
            return have(p, t, m, r, piece) + core_in[p, t, m, r, rows(piece), :].astype(F32)

        def a_rows(t):
            for piece in (A0, A1):
                for m in range(4):
                    value = core_sum(t, m, BOTH, piece)
                    if m in (FIRST[piece], FIRST[piece] + 1):
                        pack(p, t, m, BOTH, piece, value)
                    else:
                        keep(p, t, m, BOTH, piece, value)

        def b_far():
            for m in range(4):
                value = core_sum(FAR, m, BOTH, B)
                pack(p, FAR, m, BOTH, B, value)
                keep(p, FAR, m, BOTH, B, value)

        def b_near():
            for m in range(4):
                pack(p, NEAR, m, 1, B, core_sum(NEAR, m, 1, B))
                keep(p, NEAR, m, 0, B, core_sum(NEAR, m, 0, B))

        when(section != 2, lambda: arrived((p, "core", FAR), core_in.at[p, FAR]))
        b_far()
        send(None, (p, "b side"), out(p, FAR, ALL, xh, B0), slot(0, p, FAR, ALL, 1 - xh, B0), x_side)
        for r in range(2):
            send(near_here, (p, "b cross", 1 - r), out(p, FAR, ALL, r, B1), slot(0, p, FAR, ALL, 1 - r, B1), x_cross)
        a_rows(FAR)
        for piece in (A0, A1):
            y_one(None, (p, "a y1", FAR, piece), 0, p, FAR, BOTH, piece)
        when(section == 1, lambda: arrived((p, "core", NEAR), core_in.at[p, NEAR]))
        when(near_here, b_near)
        send(near_here, (p, "b near"), out(p, NEAR, ALL, 1, B), slot(0, p, NEAR, ALL, 0, B), x_side)
        when(near_here, lambda: a_rows(NEAR))
        for piece in (A0, A1):
            y_one(near_here, (p, "a y1", NEAR, piece), 0, p, NEAR, BOTH, piece)

    def a_second(p, t, cond):
        for piece in (A0, A1):
            key = (p, "a y1", t, piece)
            k = Y_PATH[piece][1]
            s = SLOT_OF[piece].index(k)

            def go():
                arrived(key, got.at[0, p, t, BOTH, BOTH, rows(piece), :])
                pack(p, t, k, BOTH, piece, have(p, t, k, BOTH, piece) + came(0, p, t, s, BOTH, piece))

            when(cond, go)
            y_two(cond, (p, "a y2", t, piece), 1, p, t, BOTH, piece)

    def b_y_first(p, t, cond):
        for piece in (B0, B1):
            when(cond, lambda: [pack(p, t, m, 0, piece, have(p, t, m, 0, piece)) for m in (FIRST[piece], FIRST[piece] + 1)])
            y_one(cond, (p, "b y1", piece), 2, p, t, 0, piece)

    def b_y_second(p, t, cond):
        for piece in (B0, B1):
            k = Y_PATH[piece][1]
            s = SLOT_OF[piece].index(k)

            def go():
                arrived((p, "b y1", piece), got.at[2, p, t, BOTH, 0, rows(piece), :])
                pack(p, t, k, 0, piece, have(p, t, k, 0, piece) + came(2, p, t, s, 0, piece))

            when(cond, go)
            y_two(cond, (p, "b y2", piece), 3, p, t, 0, piece)

    def b_final(p, t):
        total = []
        for piece in (B0, B1):
            arrived((p, "b y2", piece), slot(3, p, t, 0, 0, piece))
            s = SLOT_OF[piece].index(0)
            total.append(have(p, t, 0, 0, piece) + came(2, p, t, s, 0, piece) + came(3, p, t, 0, 0, piece))
        return total

    def a_y_sum(p, t, piece, r):
        s = SLOT_OF[piece].index(0)
        return have(p, t, 0, r, piece) + came(0, p, t, s, r, piece) + came(1, p, t, 0, r, piece)

    def second(p):
        arrived((p, "b side"), slot(0, p, FAR, ALL, 1 - xh, B0))

        def far_near():
            pack(p, FAR, ALL, 1, B0, have(p, FAR, ALL, 1, B0) + came(0, p, FAR, ALL, 1, B0))

        def far_far():
            keep(p, FAR, ALL, 0, B0, have(p, FAR, ALL, 0, B0) + came(0, p, FAR, ALL, 0, B0))
            for r in range(2):
                arrived((p, "b cross", r), slot(0, p, FAR, ALL, r, B1))
            pack(p, FAR, ALL, 1, B1, have(p, FAR, ALL, 1, B1) + came(0, p, FAR, ALL, 1, B1))
            keep(p, FAR, ALL, 0, B1, have(p, FAR, ALL, 0, B1) + came(0, p, FAR, ALL, 0, B1))

        when(near_here, far_near)
        send(near_here, (p, "b cross2"), out(p, FAR, ALL, 1, B0), slot(1, p, FAR, ALL, 0, B0), x_cross)
        when(far_here, far_far)
        send(far_here, (p, "b side2"), out(p, FAR, ALL, 1, B1), slot(1, p, FAR, ALL, 0, B1), x_side)
        a_second(p, FAR, None)

        def near_near():
            arrived((p, "b near"), slot(0, p, NEAR, ALL, 0, B))
            keep(p, NEAR, ALL, 0, B, have(p, NEAR, ALL, 0, B) + came(0, p, NEAR, ALL, 0, B))

        when(near_here, near_near)
        b_y_first(p, NEAR, near_here)
        a_second(p, NEAR, near_here)

    def third(p):
        def b_far():
            arrived((p, "b cross2"), slot(1, p, FAR, ALL, 0, B0))
            arrived((p, "b side2"), slot(1, p, FAR, ALL, 0, B1))
            keep(p, FAR, ALL, 0, B, have(p, FAR, ALL, 0, B) + came(1, p, FAR, ALL, 0, B))

        when(far_here, b_far)
        b_y_first(p, FAR, far_here)

        for piece in (A0, A1):
            arrived((p, "a y2", FAR, piece), slot(1, p, FAR, 0, BOTH, piece))
            value = a_y_sum(p, FAR, piece, BOTH)
            pack(p, FAR, 0, BOTH, piece, value)
            keep(p, FAR, 0, BOTH, piece, value)
        send(None, (p, "a side"), out(p, FAR, 0, xh, A0), slot(2, p, FAR, 0, 1 - xh, A0), x_side)
        for r in range(2):
            send(near_here, (p, "a cross", 1 - r), out(p, FAR, 0, r, A1), slot(2, p, FAR, 0, 1 - r, A1), x_cross)

        def a_near():
            for piece in (A0, A1):
                arrived((p, "a y2", NEAR, piece), slot(1, p, NEAR, 0, BOTH, piece))
                pack(p, NEAR, 0, 1, piece, a_y_sum(p, NEAR, piece, 1))
                keep(p, NEAR, 0, 0, piece, a_y_sum(p, NEAR, piece, 0))

        when(near_here, a_near)
        send(near_here, (p, "a near"), out(p, NEAR, 0, 1, A), slot(2, p, NEAR, 0, 0, A), x_side)
        b_y_second(p, NEAR, near_here)

    def hand_on(p, cond, parts):
        def turn():
            whole = jnp.concatenate(parts(), axis=0).T.reshape(2, 64, TOK)
            z_out[p] = whole.astype(BF16)
            if p == 0:
                z_own[...] = whole

        when(cond, turn)
        for e in range(2):
            if (p, e) in z_by:
                send(cond, (p, "z", e), z_out.at[p, z_low if e == 0 else 1 - z_low], z_in.at[p, e], z_by[(p, e)])

    def fourth(p):
        arrived((p, "a side"), slot(2, p, FAR, 0, 1 - xh, A0))

        def far_near():
            pack(p, FAR, 0, 1, A0, have(p, FAR, 0, 1, A0) + came(2, p, FAR, 0, 1, A0))

        def far_far():
            keep(p, FAR, 0, 0, A0, have(p, FAR, 0, 0, A0) + came(2, p, FAR, 0, 0, A0))
            for r in range(2):
                arrived((p, "a cross", r), slot(2, p, FAR, 0, r, A1))
            pack(p, FAR, 0, 1, A1, have(p, FAR, 0, 1, A1) + came(2, p, FAR, 0, 1, A1))
            keep(p, FAR, 0, 0, A1, have(p, FAR, 0, 0, A1) + came(2, p, FAR, 0, 0, A1))

        when(near_here, far_near)
        send(near_here, (p, "a cross2"), out(p, FAR, 0, 1, A0), slot(3, p, FAR, 0, 0, A0), x_cross)
        when(far_here, far_far)
        send(far_here, (p, "a side2"), out(p, FAR, 0, 1, A1), slot(3, p, FAR, 0, 0, A1), x_side)
        b_y_second(p, FAR, far_here)

        def near_parts():
            arrived((p, "a near"), slot(2, p, NEAR, 0, 0, A))
            return [have(p, NEAR, 0, 0, A) + came(2, p, NEAR, 0, 0, A)] + b_final(p, NEAR)

        hand_on(p, near_here, near_parts)

    def fifth(p):
        def far_parts():
            arrived((p, "a cross2"), slot(3, p, FAR, 0, 0, A0))
            arrived((p, "a side2"), slot(3, p, FAR, 0, 0, A1))
            return [have(p, FAR, 0, 0, A) + came(3, p, FAR, 0, 0, A)] + b_final(p, FAR)

        hand_on(p, far_here, far_parts)

    pl.semaphore_wait(barrier, 12)
    t0, t1, t2, t3 = TILES
    for stage, p in (
        (multiply, t0), (multiply, t1), (first, t0), (multiply, t2), (first, t1), (multiply, t3),
        (second, t0), (first, t2), (third, t0), (second, t1), (first, t3), (fourth, t0), (third, t1), (second, t2),
        (fifth, t0), (fourth, t1), (third, t2), (second, t3), (fifth, t1), (fourth, t2), (third, t3),
        (fifth, t2), (fourth, t3), (fifth, t3),
    ):
        stage(p)

    total = z_own[z_low]
    for p in TILES:
        for e in range(2):
            if (p, e) in z_by:
                arrived((p, "z", e), z_in.at[p, e])
                total = total + z_in[p, e].astype(F32)
    out_ref[0] = total.astype(BF16)

    for cond, key, src, dst, peer in pending:
        when(cond, lambda: remote(key, src, dst, peer).wait_send())


def local(residual, enc_weight, dec_weight, latent_ids):
    dec = dec_weight[0].reshape(256, 4, 32, 128).transpose(0, 2, 1, 3).reshape(256, 32, 2, 2, 128)
    ids = latent_ids.transpose(0, 2, 1)
    blocks = (4, 2, 4, 2, TOK, 128)
    return pl.pallas_call(
        kernel,
        out_shape=jax.ShapeDtypeStruct((1, 64, TOK), BF16),
        in_specs=[pl.BlockSpec(memory_space=pl.ANY)] * 4,
        out_specs=pl.BlockSpec(memory_space=pltpu.VMEM),
        scratch_shapes=[
            pltpu.VMEM((TOK, 4096), BF16),
            pltpu.VMEM((4096, 256), BF16),
            pltpu.VMEM((64, TOK), jnp.int32),
            pltpu.VMEM((4, 2, 4, 2, 256, 2, 128), BF16),
            pltpu.VMEM((2, 2 * TOK, 512), BF16),
            pltpu.VMEM(blocks, F32),
            pltpu.VMEM(blocks, BF16),
            pltpu.VMEM(blocks, BF16),
            pltpu.VMEM(blocks, BF16),
            pltpu.VMEM((4,) + blocks, BF16),
            pltpu.VMEM((2, 64, TOK), F32),
            pltpu.VMEM((4, 2, 64, TOK), BF16),
            pltpu.VMEM((4, 2, 64, TOK), BF16),
            pltpu.SemaphoreType.DMA((72,)),
            pltpu.SemaphoreType.DMA((128,)),
            pltpu.SemaphoreType.DMA((128,)),
        ],
        compiler_params=pltpu.CompilerParams(
            collective_id=0, has_side_effects=True, vmem_limit_bytes=60 * 1024 * 1024
        ),
    )(residual, enc_weight, dec, ids)


def solution(mesh):
    in_specs = (
        P("section", None, None),
        P("section", None, "feat"),
        P("section", "feat", None, None),
        P("section", None, None),
    )
    return jax.shard_map(local, mesh=mesh, in_specs=in_specs, out_specs=P("section", "feat", None), check_vma=False)
```

```python
import jax
import jax.numpy as jnp
from jax import lax
from jax.experimental import pallas as pl
from jax.experimental.pallas import tpu as pltpu
from jax.sharding import PartitionSpec as P

MESH = pl.DeviceIdType.MESH
F32, BF16 = jnp.float32, jnp.bfloat16
TOK = 128
A, B = (0, 64), (64, 64)
NEAR, FAR = 0, 1
TILES = (2, 1, 3, 0)


def when(cond, run):
    if cond is None:
        run()
    else:
        @pl.when(cond)
        def _():
            run()


def rows(piece):
    return pl.ds(piece[0], piece[1])


def kernel(res_hbm, enc_hbm, dec_hbm, ids_hbm, out_ref, res, enc, ids, dec, lhs, acc, core_out, core_in, sent, got,
           z_own, z_out, z_in, load_sem, send_sem, recv_sem):
    section, feat = lax.axis_index("section"), lax.axis_index("feat")
    core, xh = section % 2, section // 2
    y, xl, z = feat // 16, (feat // 8) % 2, feat % 8
    z_pair, z_low = z // 2, z % 2
    flip = {0: y, 1: y + 1 - 2 * (y % 2), 2: (y + 2) % 4, 3: 3 - y}
    near_here, far_here = xh == 0, xh == 1

    def device(core_=core, xh_=xh, y_=y, xl_=xl, z_=z):
        return (xh_ * 2 + core_, (y_ * 2 + xl_) * 8 + z_)

    other_core = device(core_=1 - core)
    y_by = {m: device(y_=flip[m]) for m in range(1, 4)}
    x_side = device(xl_=1 - xl)
    x_cross = device(xh_=1 - xh, xl_=1 - xl)
    x_straight = device(xh_=1 - xh)
    tile_of = {p: (z_pair + p) % 4 for p in TILES}
    z_by = {(p, e): device(z_=2 * tile_of[p] + (z_low if e == 0 else 1 - z_low)) for p in TILES for e in range(2)}
    z_by.pop((0, 0))

    barrier = pltpu.get_barrier_semaphore()
    for peer in [other_core, y_by[1], y_by[2], y_by[3], x_side, x_cross, x_straight] + list(z_by.values()):
        pl.semaphore_signal(barrier, inc=1, device_id=peer, device_id_type=MESH)

    loads = {}

    def load(key, src, dst):
        copy = pltpu.make_async_copy(src, dst, load_sem.at[len(loads)])
        loads[key] = copy
        return copy

    def load_dec(p, t):
        for m in range(4):
            for r in range(2):
                tile = flip[m] * 8 + (xl if r == 0 else 1 - xl) * 4 + tile_of[p]
                load((p, t, m, r), dec_hbm.at[:, tile, t], dec.at[p, t, m, r])
        when(near_here if t == NEAR else None, lambda: [loads[(p, t, m, r)].start() for m in range(4) for r in range(2)])

    load("ids", ids_hbm.at[0], ids).start()
    load("res", res_hbm.at[0], res).start()
    load("enc", enc_hbm.at[0], enc).start()
    for p in TILES:
        load_dec(p, FAR)
        load_dec(p, NEAR)

    for nothing_comes, t in ((section == 0, NEAR), (section == 2, FAR)):
        @pl.when(nothing_comes)
        def _():
            for p in TILES:
                core_in[p, t] = jnp.zeros((4, 2, TOK, 128), BF16)

    loads["ids"].wait()
    local_ids = ids[...] - feat * 256
    latent = lax.broadcasted_iota(jnp.int32, (256, TOK), 0)
    active = latent == local_ids[0:1, :]
    for k in range(1, 64):
        active = active | (latent == local_ids[k:k + 1, :])
    active = jnp.where(active, 1.0, 0.0).astype(F32).T
    spread = (lax.broadcasted_iota(jnp.int32, (256, 512), 1) // 2 == lax.broadcasted_iota(jnp.int32, (256, 512), 0))
    spread = jnp.where(spread, 1.0, 0.0).astype(BF16)
    loads["res"].wait()
    loads["enc"].wait()
    pre_acts = jnp.dot(res[...], enc[...], preferred_element_type=F32)
    acts = (jnp.maximum(pre_acts, 0.0) * active).astype(BF16)
    acts = jnp.dot(acts, spread, preferred_element_type=F32).astype(BF16)
    place = lax.broadcasted_iota(jnp.int32, (TOK, 512), 1) % 2
    for t in range(2):
        for row, low in enumerate((1 - core, core)):
            keep = (place == low) & (2 * t + low >= section)
            lhs[t, pl.ds(row * TOK, TOK), :] = jnp.where(keep, acts, jnp.zeros_like(acts))

    numbers = {}
    pending = []

    def remote(key, src, dst, peer):
        i = numbers.setdefault(key, len(numbers))
        return pltpu.make_async_remote_copy(
            src_ref=src, dst_ref=dst, send_sem=send_sem.at[i], recv_sem=recv_sem.at[i], device_id=peer, device_id_type=MESH
        )

    def send(cond, key, src, dst, peer):
        when(cond, lambda: remote(key, src, dst, peer).start())
        pending.append((cond, key, src, dst, peer))

    def arrived(key, region):
        remote(key, region, region, other_core).wait_recv()

    ALL, BOTH = pl.ds(0, 4), pl.ds(0, 2)

    def out(p, t, m, r, piece):
        return sent.at[p, t, m, r, rows(piece), :]

    def slot(step, p, t, m, r, piece):
        return got.at[step, p, t, m, r, rows(piece), :]

    def have(p, t, m, r, piece):
        return acc[p, t, m, r, rows(piece), :]

    def came(step, p, t, m, r, piece):
        return got[step, p, t, m, r, rows(piece), :].astype(F32)

    def keep(p, t, m, r, piece, value):
        acc[p, t, m, r, rows(piece), :] = value

    def pack(p, t, m, r, piece, value):
        sent[p, t, m, r, rows(piece), :] = value.astype(BF16)

    def multiply(p):
        def one(t):
            for m in range(4):
                for r in range(2):
                    loads[(p, t, m, r)].wait()
            for m in range(4):
                w = jnp.concatenate([dec.at[p, t, m, r].reshape(512, 128)[...] for r in range(2)], axis=1)
                both = jnp.dot(lhs[t], w, preferred_element_type=F32)
                for r in range(2):
                    core_out[p, t, m, r] = both[0:TOK, r * 128:(r + 1) * 128].astype(BF16)
                    acc[p, t, m, r] = both[TOK:2 * TOK, r * 128:(r + 1) * 128]

        one(FAR)
        send(section != 3, (p, "core", FAR), core_out.at[p, FAR], core_in.at[p, FAR], other_core)
        when(near_here, lambda: one(NEAR))
        send(section == 0, (p, "core", NEAR), core_out.at[p, NEAR], core_in.at[p, NEAR], other_core)

    def first(p):
        def core_sum(t, m, r, piece):
            return have(p, t, m, r, piece) + core_in[p, t, m, r, rows(piece), :].astype(F32)

        def a_rows(t):
            for m in range(1, 4):
                pack(p, t, m, BOTH, A, core_sum(t, m, BOTH, A))
            keep(p, t, 0, BOTH, A, core_sum(t, 0, BOTH, A))

        def b_rows(t):
            for m in range(4):
                pack(p, t, m, 1, B, core_sum(t, m, 1, B))
            if t == NEAR:
                for m in range(4):
                    keep(p, t, m, 0, B, core_sum(t, m, 0, B))
            else:
                @pl.when(near_here)
                def _():
                    for m in range(4):
                        pack(p, t, m, 0, B, core_sum(t, m, 0, B))

                @pl.when(far_here)
                def _():
                    for m in range(4):
                        keep(p, t, m, 0, B, core_sum(t, m, 0, B))

        def y_out(cond, t):
            for m in (2, 1, 3):
                send(cond, (p, "a y", t, m), out(p, t, m, BOTH, A), slot(0, p, t, m, BOTH, A), y_by[m])

        when(section != 2, lambda: arrived((p, "core", FAR), core_in.at[p, FAR]))
        b_rows(FAR)
        x_out(p, "b", FAR, ALL, B, (0, 1, 2))
        a_rows(FAR)
        y_out(None, FAR)
        when(section == 1, lambda: arrived((p, "core", NEAR), core_in.at[p, NEAR]))
        when(near_here, lambda: b_rows(NEAR))
        x_out(p, "b", NEAR, ALL, B, (0, 1, 2))
        when(near_here, lambda: a_rows(NEAR))
        y_out(near_here, NEAR)

    def x_out(p, name, t, m, piece, steps):
        side, cross, straight = steps
        if t == NEAR:
            send(near_here, (p, name, "near"), out(p, t, m, 1, piece), slot(side, p, t, m, 0, piece), x_side)
        else:
            send(near_here, (p, name, "straight"), out(p, t, m, 0, piece), slot(straight, p, t, m, 0, piece), x_straight)
            send(near_here, (p, name, "cross"), out(p, t, m, 1, piece), slot(cross, p, t, m, 0, piece), x_cross)
            send(far_here, (p, name, "side"), out(p, t, m, 1, piece), slot(side, p, t, m, 0, piece), x_side)

    def x_in(p, name, t, m, piece, steps):
        side, cross, straight = steps
        if t == NEAR:
            arrived((p, name, "near"), slot(side, p, t, m, 0, piece))
        else:
            arrived((p, name, "side"), slot(side, p, t, m, 0, piece))
            arrived((p, name, "cross"), slot(cross, p, t, m, 0, piece))
            arrived((p, name, "straight"), slot(straight, p, t, m, 0, piece))

    def x_sum(p, t, m, piece, steps):
        value = have(p, t, m, 0, piece)
        for step in steps[:1] if t == NEAR else steps:
            value = value + came(step, p, t, m, 0, piece)
        return value

    def second(p):
        def b_own(t):
            x_in(p, "b", t, ALL, B, (0, 1, 2))
            for m in range(1, 4):
                pack(p, t, m, 0, B, x_sum(p, t, m, B, (0, 1, 2)))
            keep(p, t, 0, 0, B, x_sum(p, t, 0, B, (0, 1, 2)))

        def a_sum(t, r):
            value = have(p, t, 0, r, A)
            for m in range(1, 4):
                value = value + came(0, p, t, m, r, A)
            return value

        def a_in(t):
            for m in range(1, 4):
                arrived((p, "a y", t, m), slot(0, p, t, m, BOTH, A))

        def a_far():
            a_in(FAR)
            pack(p, FAR, 0, 1, A, a_sum(FAR, 1))
            when(near_here, lambda: pack(p, FAR, 0, 0, A, a_sum(FAR, 0)))
            when(far_here, lambda: keep(p, FAR, 0, 0, A, a_sum(FAR, 0)))

        def a_near():
            a_in(NEAR)
            pack(p, NEAR, 0, 1, A, a_sum(NEAR, 1))
            keep(p, NEAR, 0, 0, A, a_sum(NEAR, 0))

        def y_out(cond, t):
            for m in (2, 1, 3):
                send(cond, (p, "b y", m), out(p, t, m, 0, B), slot(3, p, t, m, 0, B), y_by[m])

        a_far()
        x_out(p, "a", FAR, 0, A, (1, 2, 3))
        when(far_here, lambda: b_own(FAR))
        y_out(far_here, FAR)
        when(near_here, lambda: b_own(NEAR))
        y_out(near_here, NEAR)
        when(near_here, a_near)
        x_out(p, "a", NEAR, 0, A, (1, 2, 3))

    def third(p):
        def parts(t):
            x_in(p, "a", t, 0, A, (1, 2, 3))
            upper = x_sum(p, t, 0, A, (1, 2, 3))
            lower = have(p, t, 0, 0, B)
            for m in range(1, 4):
                arrived((p, "b y", m), slot(3, p, t, m, 0, B))
                lower = lower + came(3, p, t, m, 0, B)
            whole = jnp.concatenate([upper, lower], axis=0).T.reshape(2, 64, TOK)
            z_out[p] = whole.astype(BF16)
            if p == 0:
                z_own[...] = whole

        when(near_here, lambda: parts(NEAR))
        when(far_here, lambda: parts(FAR))
        for e in range(2):
            if (p, e) in z_by:
                send(None, (p, "z", e), z_out.at[p, z_low if e == 0 else 1 - z_low], z_in.at[p, e], z_by[(p, e)])

    pl.semaphore_wait(barrier, 14)
    t0, t1, t2, t3 = TILES
    for stage, p in (
        (multiply, t0), (multiply, t1), (first, t0), (multiply, t2), (first, t1), (multiply, t3), (first, t2), (first, t3),
        (second, t0), (second, t1), (second, t2), (third, t0), (second, t3), (third, t1), (third, t2), (third, t3),
    ):
        stage(p)

    total = z_own[z_low]
    for p in TILES:
        for e in range(2):
            if (p, e) in z_by:
                arrived((p, "z", e), z_in.at[p, e])
                total = total + z_in[p, e].astype(F32)
    out_ref[0] = total.astype(BF16)

    for cond, key, src, dst, peer in pending:
        when(cond, lambda: remote(key, src, dst, peer).wait_send())


def local(residual, enc_weight, dec_weight, latent_ids):
    dec = dec_weight[0].reshape(256, 4, 32, 128).transpose(0, 2, 1, 3).reshape(256, 32, 2, 2, 128)
    ids = latent_ids.transpose(0, 2, 1)
    blocks = (4, 2, 4, 2, TOK, 128)
    return pl.pallas_call(
        kernel,
        out_shape=jax.ShapeDtypeStruct((1, 64, TOK), BF16),
        in_specs=[pl.BlockSpec(memory_space=pl.ANY)] * 4,
        out_specs=pl.BlockSpec(memory_space=pltpu.VMEM),
        scratch_shapes=[
            pltpu.VMEM((TOK, 4096), BF16),
            pltpu.VMEM((4096, 256), BF16),
            pltpu.VMEM((64, TOK), jnp.int32),
            pltpu.VMEM((4, 2, 4, 2, 256, 2, 128), BF16),
            pltpu.VMEM((2, 2 * TOK, 512), BF16),
            pltpu.VMEM(blocks, F32),
            pltpu.VMEM(blocks, BF16),
            pltpu.VMEM(blocks, BF16),
            pltpu.VMEM(blocks, BF16),
            pltpu.VMEM((4,) + blocks, BF16),
            pltpu.VMEM((2, 64, TOK), F32),
            pltpu.VMEM((4, 2, 64, TOK), BF16),
            pltpu.VMEM((4, 2, 64, TOK), BF16),
            pltpu.SemaphoreType.DMA((72,)),
            pltpu.SemaphoreType.DMA((128,)),
            pltpu.SemaphoreType.DMA((128,)),
        ],
        compiler_params=pltpu.CompilerParams(
            collective_id=0, has_side_effects=True, vmem_limit_bytes=60 * 1024 * 1024
        ),
    )(residual, enc_weight, dec, ids)


def solution(mesh):
    in_specs = (
        P("section", None, None),
        P("section", None, "feat"),
        P("section", "feat", None, None),
        P("section", None, None),
    )
    return jax.shard_map(local, mesh=mesh, in_specs=in_specs, out_specs=P("section", "feat", None), check_vma=False)
```

```python
import jax
import jax.numpy as jnp
from jax import lax
from jax.experimental import pallas as pl
from jax.experimental.pallas import tpu as pltpu
from jax.sharding import PartitionSpec as P

MESH = pl.DeviceIdType.MESH
F32, BF16 = jnp.float32, jnp.bfloat16
TOK = 128
A, B = ((0, 48), (0, 80)), ((48, 80), (80, 48))
SPLIT = (((0, 16), (16, 32)), ((0, 48), (48, 32)))
NEAR, FAR = 0, 1
TILES = (2, 1, 3, 0)


def when(cond, run):
    if cond is None:
        run()
    else:
        @pl.when(cond)
        def _():
            run()


def rows(piece):
    return pl.ds(piece[0], piece[1])


def kernel(res_hbm, enc_hbm, dec_hbm, ids_hbm, out_ref, res, enc, ids, dec, lhs, acc, core_out, core_in, sent, got,
           z_own, z_out, z_in, load_sem, send_sem, recv_sem):
    section, feat = lax.axis_index("section"), lax.axis_index("feat")
    core, xh = section % 2, section // 2
    y, xl, z = feat // 16, (feat // 8) % 2, feat % 8
    z_pair, z_low = z // 2, z % 2
    flip = {0: y, 1: y + 1 - 2 * (y % 2), 2: (y + 2) % 4, 3: 3 - y}
    near_here, far_here = xh == 0, xh == 1

    def device(core_=core, xh_=xh, y_=y, xl_=xl, z_=z):
        return (xh_ * 2 + core_, (y_ * 2 + xl_) * 8 + z_)

    other_core = device(core_=1 - core)
    y_by = {m: device(y_=flip[m]) for m in range(1, 4)}
    x_side = device(xl_=1 - xl)
    x_cross = device(xh_=1 - xh, xl_=1 - xl)
    x_straight = device(xh_=1 - xh)
    tile_of = {p: (z_pair + p) % 4 for p in TILES}
    z_by = {(p, e): device(z_=2 * tile_of[p] + (z_low if e == 0 else 1 - z_low)) for p in TILES for e in range(2)}
    z_by.pop((0, 0))

    barrier = pltpu.get_barrier_semaphore()
    for peer in [other_core, y_by[1], y_by[2], y_by[3], x_side, x_cross, x_straight] + list(z_by.values()):
        pl.semaphore_signal(barrier, inc=1, device_id=peer, device_id_type=MESH)

    loads = {}

    def load(key, src, dst):
        copy = pltpu.make_async_copy(src, dst, load_sem.at[len(loads)])
        loads[key] = copy
        return copy

    def load_dec(p, t):
        for m in range(4):
            for r in range(2):
                tile = flip[m] * 8 + (xl if r == 0 else 1 - xl) * 4 + tile_of[p]
                load((p, t, m, r), dec_hbm.at[:, tile, t], dec.at[p, t, m, r])
        when(near_here if t == NEAR else None, lambda: [loads[(p, t, m, r)].start() for m in range(4) for r in range(2)])

    load("ids", ids_hbm.at[0], ids).start()
    for c in range(4):
        part = pl.ds(c * 1024, 1024)
        load(("res", c), res_hbm.at[0, :, part], res.at[:, part]).start()
        load(("enc", c), enc_hbm.at[0, part, :], enc.at[part, :]).start()
    for p in TILES:
        load_dec(p, FAR)
        load_dec(p, NEAR)

    loads["ids"].wait()
    local_ids = ids[...] - feat * 256
    latent = lax.broadcasted_iota(jnp.int32, (256, TOK), 0)
    active = latent == local_ids[0:1, :]
    for k in range(1, 64):
        active = active | (latent == local_ids[k:k + 1, :])
    active = jnp.where(active, 1.0, 0.0).astype(F32).T
    spread = (lax.broadcasted_iota(jnp.int32, (256, 512), 1) // 2 == lax.broadcasted_iota(jnp.int32, (256, 512), 0))
    spread = jnp.where(spread, 1.0, 0.0).astype(BF16)
    pre_acts = jnp.zeros((TOK, 256), F32)
    for c in range(4):
        part = pl.ds(c * 1024, 1024)
        loads[("res", c)].wait()
        loads[("enc", c)].wait()
        pre_acts = pre_acts + jnp.dot(res[:, part], enc[part, :], preferred_element_type=F32)
    acts = (jnp.maximum(pre_acts, 0.0) * active).astype(BF16)
    acts = jnp.dot(acts, spread, preferred_element_type=F32).astype(BF16)
    place = lax.broadcasted_iota(jnp.int32, (TOK, 512), 1) % 2
    for t in range(2):
        for row, low in enumerate((1 - core, core)):
            keep = (place == low) & (2 * t + low >= section)
            lhs[t, pl.ds(row * TOK, TOK), :] = jnp.where(keep, acts, jnp.zeros_like(acts))

    numbers = {}
    pending = []

    def remote(key, src, dst, peer):
        i = numbers.setdefault(key, len(numbers))
        return pltpu.make_async_remote_copy(
            src_ref=src, dst_ref=dst, send_sem=send_sem.at[i], recv_sem=recv_sem.at[i], device_id=peer, device_id_type=MESH
        )

    def send(cond, key, src, dst, peer):
        when(cond, lambda: remote(key, src, dst, peer).start())
        pending.append((cond, key, src, dst, peer))

    def arrived(key, region):
        remote(key, region, region, other_core).wait_recv()

    ALL, BOTH = pl.ds(0, 4), pl.ds(0, 2)

    def out(p, t, m, r, piece):
        return sent.at[p, t, m, r, rows(piece), :]

    def slot(step, p, t, m, r, piece):
        return got.at[step, p, t, m, r, rows(piece), :]

    def have(p, t, m, r, piece):
        return acc[p, t, m, r, rows(piece), :]

    def came(step, p, t, m, r, piece):
        return got[step, p, t, m, r, rows(piece), :].astype(F32)

    def keep(p, t, m, r, piece, value):
        acc[p, t, m, r, rows(piece), :] = value

    def pack(p, t, m, r, piece, value):
        sent[p, t, m, r, rows(piece), :] = value.astype(BF16)

    def multiply(p, far):
        def one(t):
            for m in range(4):
                for r in range(2):
                    loads[(p, t, m, r)].wait()
            for m in range(4):
                w = jnp.concatenate([dec.at[p, t, m, r].reshape(512, 128)[...] for r in range(2)], axis=1)
                both = jnp.dot(lhs[t], w, preferred_element_type=F32)
                for r in range(2):
                    core_out[p, t, m, r] = both[0:TOK, r * 128:(r + 1) * 128].astype(BF16)
                    acc[p, t, m, r] = both[TOK:2 * TOK, r * 128:(r + 1) * 128]

        if far:
            one(FAR)
            send(section != 3, (p, "core", FAR), core_out.at[p, FAR], core_in.at[p, FAR], other_core)
            return
        when(near_here, lambda: one(NEAR))
        send(section == 0, (p, "core", NEAR), core_out.at[p, NEAR], core_in.at[p, NEAR], other_core)

    PATHS = ((1, 1, 3), (3, 2, 1))
    SLOT_OF = ((0, 3), (1, 0))

    def halving(p):
        return p != 0

    def a_rows(p, t, core_sum):
        if not halving(p):
            for m in range(1, 4):
                pack(p, t, m, BOTH, A[t], core_sum(t, m, BOTH, A[t]))
            keep(p, t, 0, BOTH, A[t], core_sum(t, 0, BOTH, A[t]))
            return
        for path, piece in zip(PATHS, SPLIT[t]):
            for m in range(4):
                (pack if m in (path[1], path[1] + 1) else keep)(p, t, m, BOTH, piece, core_sum(t, m, BOTH, piece))

    def a_y_out(p, cond, t):
        if not halving(p):
            for m in (2, 1, 3):
                send(cond, (p, "a y", t, m), out(p, t, m, BOTH, A[t]), slot(0, p, t, m, BOTH, A[t]), y_by[m])
            return
        for path, piece in zip(PATHS, SPLIT[t]):
            send(cond, (p, "a y1", t, path), sent.at[p, t, pl.ds(path[1], 2), BOTH, rows(piece), :],
                 got.at[0, p, t, BOTH, BOTH, rows(piece), :], y_by[path[0]])

    def middle(p):
        def one(t):
            for path, piece, slots in zip(PATHS, SPLIT[t], SLOT_OF):
                k = path[2]
                arrived((p, "a y1", t, path), got.at[0, p, t, BOTH, BOTH, rows(piece), :])
                pack(p, t, k, BOTH, piece, have(p, t, k, BOTH, piece) + came(0, p, t, slots.index(k), BOTH, piece))

        for t, cond in ((FAR, None), (NEAR, near_here)):
            when(cond, lambda: one(t))
            for path, piece in zip(PATHS, SPLIT[t]):
                k = path[2]
                send(cond, (p, "a y2", t, path), out(p, t, k, BOTH, piece), slot(0, p, t, 3, BOTH, piece), y_by[k])

    def a_in(p, t):
        if not halving(p):
            for m in range(1, 4):
                arrived((p, "a y", t, m), slot(0, p, t, m, BOTH, A[t]))
            return
        for path, piece in zip(PATHS, SPLIT[t]):
            arrived((p, "a y2", t, path), slot(0, p, t, 3, BOTH, piece))

    def a_each(p, t, r, put):
        if not halving(p):
            value = have(p, t, 0, r, A[t])
            for m in range(1, 4):
                value = value + came(0, p, t, m, r, A[t])
            put(p, t, 0, r, A[t], value)
            return
        for piece, slots in zip(SPLIT[t], SLOT_OF):
            value = have(p, t, 0, r, piece) + came(0, p, t, slots.index(0), r, piece) + came(0, p, t, 3, r, piece)
            put(p, t, 0, r, piece, value)

    def first(p, far):
        def nothing_came(t):
            core_in[p, t] = jnp.zeros((4, 2, TOK, 128), BF16)

        def core_sum(t, m, r, piece):
            return have(p, t, m, r, piece) + core_in[p, t, m, r, rows(piece), :].astype(F32)

        def b_rows(t):
            for m in range(4):
                pack(p, t, m, 1, B[t], core_sum(t, m, 1, B[t]))
            if t == NEAR:
                for m in range(4):
                    keep(p, t, m, 0, B[t], core_sum(t, m, 0, B[t]))
            else:
                @pl.when(near_here)
                def _():
                    for m in range(4):
                        pack(p, t, m, 0, B[t], core_sum(t, m, 0, B[t]))

                @pl.when(far_here)
                def _():
                    for m in range(4):
                        keep(p, t, m, 0, B[t], core_sum(t, m, 0, B[t]))

        if far:
            when(section != 2, lambda: arrived((p, "core", FAR), core_in.at[p, FAR]))
            when(section == 2, lambda: nothing_came(FAR))
            b_rows(FAR)
            x_out(p, "b", FAR, ALL, B[FAR], (0, 1, 2))
            a_rows(p, FAR, core_sum)
            a_y_out(p, None, FAR)
            return
        when(section == 1, lambda: arrived((p, "core", NEAR), core_in.at[p, NEAR]))
        when(section == 0, lambda: nothing_came(NEAR))
        when(near_here, lambda: b_rows(NEAR))
        x_out(p, "b", NEAR, ALL, B[NEAR], (0, 1, 2))
        when(near_here, lambda: a_rows(p, NEAR, core_sum))
        a_y_out(p, near_here, NEAR)

    def x_out(p, name, t, m, piece, steps):
        side, cross, straight = steps
        if t == NEAR:
            send(near_here, (p, name, "near"), out(p, t, m, 1, piece), slot(side, p, t, m, 0, piece), x_side)
        else:
            send(near_here, (p, name, "straight"), out(p, t, m, 0, piece), slot(straight, p, t, m, 0, piece), x_straight)
            send(near_here, (p, name, "cross"), out(p, t, m, 1, piece), slot(cross, p, t, m, 0, piece), x_cross)
            send(far_here, (p, name, "side"), out(p, t, m, 1, piece), slot(side, p, t, m, 0, piece), x_side)

    def x_in(p, name, t, m, piece, steps):
        side, cross, straight = steps
        if t == NEAR:
            arrived((p, name, "near"), slot(side, p, t, m, 0, piece))
        else:
            arrived((p, name, "side"), slot(side, p, t, m, 0, piece))
            arrived((p, name, "cross"), slot(cross, p, t, m, 0, piece))
            arrived((p, name, "straight"), slot(straight, p, t, m, 0, piece))

    def x_sum(p, t, m, piece, steps):
        value = have(p, t, m, 0, piece)
        for step in steps[:1] if t == NEAR else steps:
            value = value + came(step, p, t, m, 0, piece)
        return value

    def second(p):
        def b_own(t):
            x_in(p, "b", t, ALL, B[t], (0, 1, 2))
            for m in range(1, 4):
                pack(p, t, m, 0, B[t], x_sum(p, t, m, B[t], (0, 1, 2)))
            keep(p, t, 0, 0, B[t], x_sum(p, t, 0, B[t], (0, 1, 2)))

        def a_far():
            a_in(p, FAR)
            a_each(p, FAR, 1, pack)
            when(near_here, lambda: a_each(p, FAR, 0, pack))
            when(far_here, lambda: a_each(p, FAR, 0, keep))

        def a_near():
            a_in(p, NEAR)
            a_each(p, NEAR, 1, pack)
            a_each(p, NEAR, 0, keep)

        def y_out(cond, t):
            for m in (2, 1, 3):
                send(cond, (p, "b y", m), out(p, t, m, 0, B[t]), slot(3, p, t, m, 0, B[t]), y_by[m])

        a_far()
        x_out(p, "a", FAR, 0, A[FAR], (1, 2, 3))
        when(far_here, lambda: b_own(FAR))
        y_out(far_here, FAR)
        when(near_here, lambda: b_own(NEAR))
        y_out(near_here, NEAR)
        when(near_here, a_near)
        x_out(p, "a", NEAR, 0, A[NEAR], (1, 2, 3))

    def third(p):
        def parts(t):
            x_in(p, "a", t, 0, A[t], (1, 2, 3))
            upper = x_sum(p, t, 0, A[t], (1, 2, 3))
            lower = have(p, t, 0, 0, B[t])
            for m in range(1, 4):
                arrived((p, "b y", m), slot(3, p, t, m, 0, B[t]))
                lower = lower + came(3, p, t, m, 0, B[t])
            whole = jnp.concatenate([upper, lower], axis=0).T.reshape(2, 64, TOK)
            z_out[p] = whole.astype(BF16)
            if p == 0:
                z_own[...] = whole

        when(near_here, lambda: parts(NEAR))
        when(far_here, lambda: parts(FAR))
        for e in range(2):
            if (p, e) in z_by:
                send(None, (p, "z", e), z_out.at[p, z_low if e == 0 else 1 - z_low], z_in.at[p, e], z_by[(p, e)])

    pl.semaphore_wait(barrier, 14)
    t0, t1, t2, t3 = TILES
    for stage, *at in (
        (multiply, t0, True), (multiply, t0, False), (multiply, t1, True), (first, t0, True),
        (multiply, t1, False), (first, t0, False), (multiply, t2, True), (first, t1, True),
        (multiply, t2, False), (first, t1, False), (multiply, t3, True), (multiply, t3, False), (middle, t0),
        (first, t2, True), (first, t2, False), (middle, t1), (first, t3, True), (first, t3, False), (middle, t2),
        (second, t0), (second, t1), (second, t2), (third, t0), (second, t3), (third, t1), (third, t2), (third, t3),
    ):
        stage(*at)

    total = z_own[z_low]
    for p in TILES:
        for e in range(2):
            if (p, e) in z_by:
                arrived((p, "z", e), z_in.at[p, e])
                total = total + z_in[p, e].astype(F32)
    out_ref[0] = total.astype(BF16)

    for cond, key, src, dst, peer in pending:
        when(cond, lambda: remote(key, src, dst, peer).wait_send())


def local(residual, enc_weight, dec_weight, latent_ids):
    dec = dec_weight[0].reshape(256, 4, 32, 128).transpose(0, 2, 1, 3).reshape(256, 32, 2, 2, 128)
    ids = latent_ids.transpose(0, 2, 1)
    blocks = (4, 2, 4, 2, TOK, 128)
    return pl.pallas_call(
        kernel,
        out_shape=jax.ShapeDtypeStruct((1, 64, TOK), BF16),
        in_specs=[pl.BlockSpec(memory_space=pl.ANY)] * 4,
        out_specs=pl.BlockSpec(memory_space=pltpu.VMEM),
        scratch_shapes=[
            pltpu.VMEM((TOK, 4096), BF16),
            pltpu.VMEM((4096, 256), BF16),
            pltpu.VMEM((64, TOK), jnp.int32),
            pltpu.VMEM((4, 2, 4, 2, 256, 2, 128), BF16),
            pltpu.VMEM((2, 2 * TOK, 512), BF16),
            pltpu.VMEM(blocks, F32),
            pltpu.VMEM(blocks, BF16),
            pltpu.VMEM(blocks, BF16),
            pltpu.VMEM(blocks, BF16),
            pltpu.VMEM((4,) + blocks, BF16),
            pltpu.VMEM((2, 64, TOK), F32),
            pltpu.VMEM((4, 2, 64, TOK), BF16),
            pltpu.VMEM((4, 2, 64, TOK), BF16),
            pltpu.SemaphoreType.DMA((80,)),
            pltpu.SemaphoreType.DMA((128,)),
            pltpu.SemaphoreType.DMA((128,)),
        ],
        compiler_params=pltpu.CompilerParams(
            collective_id=0, has_side_effects=True, vmem_limit_bytes=60 * 1024 * 1024
        ),
    )(residual, enc_weight, dec, ids)


def solution(mesh):
    in_specs = (
        P("section", None, None),
        P("section", None, "feat"),
        P("section", "feat", None, None),
        P("section", None, None),
    )
    return jax.shard_map(local, mesh=mesh, in_specs=in_specs, out_specs=P("section", "feat", None), check_vma=False)
```

```python
import jax
import jax.numpy as jnp
from jax import lax
from jax.experimental import pallas as pl
from jax.experimental.pallas import tpu as pltpu
from jax.sharding import PartitionSpec as P

MESH = pl.DeviceIdType.MESH
F32, BF16 = jnp.float32, jnp.bfloat16
TOK = 128
A, B = ((0, 48), (0, 80)), ((48, 80), (80, 48))
SPLIT = (((0, 16), (16, 32)), ((0, 48), (48, 32)))
NEAR, FAR = 0, 1
TILES = (2, 1, 3, 0)


def when(cond, run):
    if cond is None:
        run()
    else:
        @pl.when(cond)
        def _():
            run()


def rows(piece):
    return pl.ds(piece[0], piece[1])


def kernel(res_hbm, enc_hbm, dec_hbm, ids_hbm, out_ref, res, enc, ids, dec, lhs, acc, core_out, core_in, sent, got,
           z_own, z_out, z_in, load_sem, send_sem, recv_sem):
    section, feat = lax.axis_index("section"), lax.axis_index("feat")
    core, xh = section % 2, section // 2
    y, xl, z = feat // 16, (feat // 8) % 2, feat % 8
    z_pair, z_low = z // 2, z % 2
    flip = {0: y, 1: y + 1 - 2 * (y % 2), 2: (y + 2) % 4, 3: 3 - y}
    near_here, far_here = xh == 0, xh == 1

    def device(core_=core, xh_=xh, y_=y, xl_=xl, z_=z):
        return (xh_ * 2 + core_, (y_ * 2 + xl_) * 8 + z_)

    other_core = device(core_=1 - core)
    y_by = {m: device(y_=flip[m]) for m in range(1, 4)}
    x_side = device(xl_=1 - xl)
    x_cross = device(xh_=1 - xh, xl_=1 - xl)
    x_straight = device(xh_=1 - xh)
    tile_of = {p: (z_pair + p) % 4 for p in TILES}
    z_by = {(p, e): device(z_=2 * tile_of[p] + (z_low if e == 0 else 1 - z_low)) for p in TILES for e in range(2)}
    z_by.pop((0, 0))

    barrier = pltpu.get_barrier_semaphore()
    for peer in [other_core, y_by[1], y_by[2], y_by[3], x_side, x_cross, x_straight] + list(z_by.values()):
        pl.semaphore_signal(barrier, inc=1, device_id=peer, device_id_type=MESH)

    loads = {}

    def load(key, src, dst):
        copy = pltpu.make_async_copy(src, dst, load_sem.at[len(loads)])
        loads[key] = copy
        return copy

    def load_dec(p, t):
        for m in range(4):
            for r in range(2):
                tile = flip[m] * 8 + (xl if r == 0 else 1 - xl) * 4 + tile_of[p]
                load((p, t, m, r), dec_hbm.at[:, tile, t], dec.at[p, t, m, r])
        when(near_here if t == NEAR else None, lambda: [loads[(p, t, m, r)].start() for m in range(4) for r in range(2)])

    load("ids", ids_hbm.at[0], ids).start()
    for c in range(4):
        part = pl.ds(c * 1024, 1024)
        load(("res", c), res_hbm.at[0, :, part], res.at[:, part]).start()
        load(("enc", c), enc_hbm.at[0, part, :], enc.at[part, :]).start()
    for p in TILES:
        load_dec(p, FAR)
        load_dec(p, NEAR)

    loads["ids"].wait()
    local_ids = ids[...] - feat * 256
    latent = lax.broadcasted_iota(jnp.int32, (256, TOK), 0)
    active = latent == local_ids[0:1, :]
    for k in range(1, 64):
        active = active | (latent == local_ids[k:k + 1, :])
    active = jnp.where(active, 1.0, 0.0).astype(F32).T
    spread = (lax.broadcasted_iota(jnp.int32, (256, 512), 1) // 2 == lax.broadcasted_iota(jnp.int32, (256, 512), 0))
    spread = jnp.where(spread, 1.0, 0.0).astype(BF16)
    pre_acts = jnp.zeros((TOK, 256), F32)
    for c in range(4):
        part = pl.ds(c * 1024, 1024)
        loads[("res", c)].wait()
        loads[("enc", c)].wait()
        pre_acts = pre_acts + jnp.dot(res[:, part], enc[part, :], preferred_element_type=F32)
    acts = (jnp.maximum(pre_acts, 0.0) * active).astype(BF16)
    acts = jnp.dot(acts, spread, preferred_element_type=F32).astype(BF16)
    place = lax.broadcasted_iota(jnp.int32, (TOK, 512), 1) % 2
    for t in range(2):
        for row, low in enumerate((1 - core, core)):
            keep = (place == low) & (2 * t + low >= section)
            lhs[t, pl.ds(row * TOK, TOK), :] = jnp.where(keep, acts, jnp.zeros_like(acts))

    numbers = {}
    pending = []

    def remote(key, src, dst, peer):
        i = numbers.setdefault(key, len(numbers))
        return pltpu.make_async_remote_copy(
            src_ref=src, dst_ref=dst, send_sem=send_sem.at[i], recv_sem=recv_sem.at[i], device_id=peer, device_id_type=MESH
        )

    def send(cond, key, src, dst, peer):
        when(cond, lambda: remote(key, src, dst, peer).start())
        pending.append((cond, key, src, dst, peer))

    def arrived(key, region):
        remote(key, region, region, other_core).wait_recv()

    ALL, BOTH = pl.ds(0, 4), pl.ds(0, 2)

    def out(p, t, m, r, piece):
        return sent.at[p, t, m, r, rows(piece), :]

    def slot(step, p, t, m, r, piece):
        return got.at[step, p, t, m, r, rows(piece), :]

    def have(p, t, m, r, piece):
        return acc[p, t, m, r, rows(piece), :]

    def came(step, p, t, m, r, piece):
        return got[step, p, t, m, r, rows(piece), :].astype(F32)

    def keep(p, t, m, r, piece, value):
        acc[p, t, m, r, rows(piece), :] = value

    def pack(p, t, m, r, piece, value):
        sent[p, t, m, r, rows(piece), :] = value.astype(BF16)

    def multiply(p, far):
        def one(t):
            for m in range(4):
                for r in range(2):
                    loads[(p, t, m, r)].wait()
            for m in range(4):
                w = jnp.concatenate([dec.at[p, t, m, r].reshape(512, 128)[...] for r in range(2)], axis=1)
                both = jnp.dot(lhs[t], w, preferred_element_type=F32)
                for r in range(2):
                    core_out[p, t, m, r] = both[0:TOK, r * 128:(r + 1) * 128].astype(BF16)
                    acc[p, t, m, r] = both[TOK:2 * TOK, r * 128:(r + 1) * 128]

        if far:
            one(FAR)
            send(section != 3, (p, "core", FAR), core_out.at[p, FAR], core_in.at[p, FAR], other_core)
            return
        when(near_here, lambda: one(NEAR))
        send(section == 0, (p, "core", NEAR), core_out.at[p, NEAR], core_in.at[p, NEAR], other_core)

    PATHS = ((1, 1, 3), (3, 2, 1))
    SLOT_OF = ((0, 3), (1, 0))

    def halving(p):
        return p != 0

    def a_rows(p, t, core_sum):
        if not halving(p):
            for m in range(1, 4):
                pack(p, t, m, BOTH, A[t], core_sum(t, m, BOTH, A[t]))
            keep(p, t, 0, BOTH, A[t], core_sum(t, 0, BOTH, A[t]))
            return
        for path, piece in zip(PATHS, SPLIT[t]):
            for m in range(4):
                (pack if m in (path[1], path[1] + 1) else keep)(p, t, m, BOTH, piece, core_sum(t, m, BOTH, piece))

    def a_y_out(p, cond, t):
        if not halving(p):
            for m in (2, 1, 3):
                send(cond, (p, "a y", t, m), out(p, t, m, BOTH, A[t]), slot(0, p, t, m, BOTH, A[t]), y_by[m])
            return
        for path, piece in zip(PATHS, SPLIT[t]):
            send(cond, (p, "a y1", t, path), sent.at[p, t, pl.ds(path[1], 2), BOTH, rows(piece), :],
                 got.at[0, p, t, BOTH, BOTH, rows(piece), :], y_by[path[0]])

    def middle(p):
        def one(t):
            for path, piece, slots in zip(PATHS, SPLIT[t], SLOT_OF):
                k = path[2]
                arrived((p, "a y1", t, path), got.at[0, p, t, BOTH, BOTH, rows(piece), :])
                pack(p, t, k, BOTH, piece, have(p, t, k, BOTH, piece) + came(0, p, t, slots.index(k), BOTH, piece))

        for t, cond in ((FAR, None), (NEAR, near_here)):
            when(cond, lambda: one(t))
            for path, piece in zip(PATHS, SPLIT[t]):
                k = path[2]
                send(cond, (p, "a y2", t, path), out(p, t, k, BOTH, piece), slot(0, p, t, 3, BOTH, piece), y_by[k])

    def a_in(p, t):
        if not halving(p):
            for m in range(1, 4):
                arrived((p, "a y", t, m), slot(0, p, t, m, BOTH, A[t]))
            return
        for path, piece in zip(PATHS, SPLIT[t]):
            arrived((p, "a y2", t, path), slot(0, p, t, 3, BOTH, piece))

    def a_each(p, t, r, put):
        if not halving(p):
            value = have(p, t, 0, r, A[t])
            for m in range(1, 4):
                value = value + came(0, p, t, m, r, A[t])
            put(p, t, 0, r, A[t], value)
            return
        for piece, slots in zip(SPLIT[t], SLOT_OF):
            value = have(p, t, 0, r, piece) + came(0, p, t, slots.index(0), r, piece) + came(0, p, t, 3, r, piece)
            put(p, t, 0, r, piece, value)

    def first(p, far):
        def nothing_came(t):
            core_in[p, t] = jnp.zeros((4, 2, TOK, 128), BF16)

        def core_sum(t, m, r, piece):
            return have(p, t, m, r, piece) + core_in[p, t, m, r, rows(piece), :].astype(F32)

        def b_rows(t):
            for m in range(4):
                pack(p, t, m, 1, B[t], core_sum(t, m, 1, B[t]))
            if t == NEAR:
                for m in range(4):
                    keep(p, t, m, 0, B[t], core_sum(t, m, 0, B[t]))
            else:
                @pl.when(near_here)
                def _():
                    for m in range(4):
                        pack(p, t, m, 0, B[t], core_sum(t, m, 0, B[t]))

                @pl.when(far_here)
                def _():
                    for m in range(4):
                        keep(p, t, m, 0, B[t], core_sum(t, m, 0, B[t]))

        if far:
            when(section != 2, lambda: arrived((p, "core", FAR), core_in.at[p, FAR]))
            when(section == 2, lambda: nothing_came(FAR))
            b_rows(FAR)
            x_out(p, "b", FAR, ALL, B[FAR], (0, 1, 2))
            a_rows(p, FAR, core_sum)
            a_y_out(p, None, FAR)
            return
        when(section == 1, lambda: arrived((p, "core", NEAR), core_in.at[p, NEAR]))
        when(section == 0, lambda: nothing_came(NEAR))
        when(near_here, lambda: b_rows(NEAR))
        x_out(p, "b", NEAR, ALL, B[NEAR], (0, 1, 2))
        when(near_here, lambda: a_rows(p, NEAR, core_sum))
        a_y_out(p, near_here, NEAR)

    def x_out(p, name, t, m, piece, steps):
        side, cross, straight = steps
        if t == NEAR:
            send(near_here, (p, name, "near"), out(p, t, m, 1, piece), slot(side, p, t, m, 0, piece), x_side)
        else:
            send(near_here, (p, name, "straight"), out(p, t, m, 0, piece), slot(straight, p, t, m, 0, piece), x_straight)
            send(near_here, (p, name, "cross"), out(p, t, m, 1, piece), slot(cross, p, t, m, 0, piece), x_cross)
            send(far_here, (p, name, "side"), out(p, t, m, 1, piece), slot(side, p, t, m, 0, piece), x_side)

    def x_in(p, name, t, m, piece, steps):
        side, cross, straight = steps
        if t == NEAR:
            arrived((p, name, "near"), slot(side, p, t, m, 0, piece))
        else:
            arrived((p, name, "side"), slot(side, p, t, m, 0, piece))
            arrived((p, name, "cross"), slot(cross, p, t, m, 0, piece))
            arrived((p, name, "straight"), slot(straight, p, t, m, 0, piece))

    def x_sum(p, t, m, piece, steps):
        value = have(p, t, m, 0, piece)
        for step in steps[:1] if t == NEAR else steps:
            value = value + came(step, p, t, m, 0, piece)
        return value

    def second(p):
        def b_own(t):
            x_in(p, "b", t, ALL, B[t], (0, 1, 2))
            for m in range(1, 4):
                pack(p, t, m, 0, B[t], x_sum(p, t, m, B[t], (0, 1, 2)))
            keep(p, t, 0, 0, B[t], x_sum(p, t, 0, B[t], (0, 1, 2)))

        def a_far():
            a_in(p, FAR)
            a_each(p, FAR, 1, pack)
            when(near_here, lambda: a_each(p, FAR, 0, pack))
            when(far_here, lambda: a_each(p, FAR, 0, keep))

        def a_near():
            a_in(p, NEAR)
            a_each(p, NEAR, 1, pack)
            a_each(p, NEAR, 0, keep)

        def y_out(cond, t):
            for m in (2, 1, 3):
                send(cond, (p, "b y", m), out(p, t, m, 0, B[t]), slot(3, p, t, m, 0, B[t]), y_by[m])

        a_far()
        x_out(p, "a", FAR, 0, A[FAR], (1, 2, 3))
        when(far_here, lambda: b_own(FAR))
        y_out(far_here, FAR)
        when(near_here, lambda: b_own(NEAR))
        y_out(near_here, NEAR)
        when(near_here, a_near)
        x_out(p, "a", NEAR, 0, A[NEAR], (1, 2, 3))

    def third(p):
        def parts(t):
            x_in(p, "a", t, 0, A[t], (1, 2, 3))
            upper = x_sum(p, t, 0, A[t], (1, 2, 3))
            lower = have(p, t, 0, 0, B[t])
            for m in range(1, 4):
                arrived((p, "b y", m), slot(3, p, t, m, 0, B[t]))
                lower = lower + came(3, p, t, m, 0, B[t])
            whole = jnp.concatenate([upper, lower], axis=0).T.reshape(2, 64, TOK)
            z_out[p] = whole.astype(BF16)
            if p == 0:
                z_own[...] = whole

        when(near_here, lambda: parts(NEAR))
        when(far_here, lambda: parts(FAR))
        for e in range(2):
            if (p, e) in z_by:
                send(None, (p, "z", e), z_out.at[p, z_low if e == 0 else 1 - z_low], z_in.at[p, e], z_by[(p, e)])

    def drain(along_z):
        for cond, key, src, dst, peer in pending:
            if (key[1] == "z") == along_z:
                when(cond, lambda: remote(key, src, dst, peer).wait_send())

    pl.semaphore_wait(barrier, 14)
    t0, t1, t2, t3 = TILES
    for stage, *at in (
        (multiply, t0, True), (multiply, t0, False), (multiply, t1, True), (first, t0, True),
        (multiply, t1, False), (first, t0, False), (multiply, t2, True), (first, t1, True),
        (multiply, t2, False), (first, t1, False), (multiply, t3, True), (multiply, t3, False), (middle, t0),
        (first, t2, True), (first, t2, False), (middle, t1), (first, t3, True), (first, t3, False), (middle, t2),
        (second, t0), (second, t1), (second, t2), (third, t0), (second, t3), (third, t1), (third, t2), (third, t3),
    ):
        if at == [t3] and stage is third:
            drain(False)
        stage(*at)

    total = z_own[z_low]
    for p in TILES:
        for e in range(2):
            if (p, e) in z_by:
                arrived((p, "z", e), z_in.at[p, e])
                total = total + z_in[p, e].astype(F32)
    out_ref[0] = total.astype(BF16)

    drain(True)


def local(residual, enc_weight, dec_weight, latent_ids):
    dec = dec_weight[0].reshape(256, 4, 32, 128).transpose(0, 2, 1, 3).reshape(256, 32, 2, 2, 128)
    ids = latent_ids.transpose(0, 2, 1)
    blocks = (4, 2, 4, 2, TOK, 128)
    return pl.pallas_call(
        kernel,
        out_shape=jax.ShapeDtypeStruct((1, 64, TOK), BF16),
        in_specs=[pl.BlockSpec(memory_space=pl.ANY)] * 4,
        out_specs=pl.BlockSpec(memory_space=pltpu.VMEM),
        scratch_shapes=[
            pltpu.VMEM((TOK, 4096), BF16),
            pltpu.VMEM((4096, 256), BF16),
            pltpu.VMEM((64, TOK), jnp.int32),
            pltpu.VMEM((4, 2, 4, 2, 256, 2, 128), BF16),
            pltpu.VMEM((2, 2 * TOK, 512), BF16),
            pltpu.VMEM(blocks, F32),
            pltpu.VMEM(blocks, BF16),
            pltpu.VMEM(blocks, BF16),
            pltpu.VMEM(blocks, BF16),
            pltpu.VMEM((4,) + blocks, BF16),
            pltpu.VMEM((2, 64, TOK), F32),
            pltpu.VMEM((4, 2, 64, TOK), BF16),
            pltpu.VMEM((4, 2, 64, TOK), BF16),
            pltpu.SemaphoreType.DMA((80,)),
            pltpu.SemaphoreType.DMA((128,)),
            pltpu.SemaphoreType.DMA((128,)),
        ],
        compiler_params=pltpu.CompilerParams(
            collective_id=0, has_side_effects=True, vmem_limit_bytes=60 * 1024 * 1024
        ),
    )(residual, enc_weight, dec, ids)


def solution(mesh):
    in_specs = (
        P("section", None, None),
        P("section", None, "feat"),
        P("section", "feat", None, None),
        P("section", None, None),
    )
    return jax.shard_map(local, mesh=mesh, in_specs=in_specs, out_specs=P("section", "feat", None), check_vma=False)
```

```python
import jax
import jax.numpy as jnp
from jax import lax
from jax.experimental import pallas as pl
from jax.experimental.pallas import tpu as pltpu
from jax.sharding import PartitionSpec as P

MESH = pl.DeviceIdType.MESH
F32, BF16 = jnp.float32, jnp.bfloat16
TOK = 128
A, B = ((0, 64), (0, 64)), ((64, 64), (64, 64))
SPLIT = (((0, 32), (32, 32)), ((0, 32), (32, 32)))
NEAR, FAR = 0, 1
TILES = (2, 1, 3, 0)


def when(cond, run):
    if cond is None:
        run()
    else:
        @pl.when(cond)
        def _():
            run()


def rows(piece):
    return pl.ds(piece[0], piece[1])


def kernel(res_hbm, enc_hbm, dec_hbm, ids_hbm, out_ref, res, enc, ids, dec, lhs, acc, core_out, core_in, sent, got,
           z_own, z_out, z_in, load_sem, send_sem, recv_sem):
    section, feat = lax.axis_index("section"), lax.axis_index("feat")
    core, xh = section % 2, section // 2
    y, xl, z = feat // 16, (feat // 8) % 2, feat % 8
    z_pair, z_low = z // 2, z % 2
    flip = {0: y, 1: y + 1 - 2 * (y % 2), 2: (y + 2) % 4, 3: 3 - y}
    near_here, far_here = xh == 0, xh == 1

    def device(core_=core, xh_=xh, y_=y, xl_=xl, z_=z):
        return (xh_ * 2 + core_, (y_ * 2 + xl_) * 8 + z_)

    other_core = device(core_=1 - core)
    y_by = {m: device(y_=flip[m]) for m in range(1, 4)}
    x_side = device(xl_=1 - xl)
    x_cross = device(xh_=1 - xh, xl_=1 - xl)
    x_straight = device(xh_=1 - xh)
    tile_of = {p: (z_pair + p) % 4 for p in TILES}
    z_by = {(p, e): device(z_=2 * tile_of[p] + (z_low if e == 0 else 1 - z_low)) for p in TILES for e in range(2)}
    z_by.pop((0, 0))

    barrier = pltpu.get_barrier_semaphore()
    for peer in [other_core, y_by[1], y_by[2], y_by[3], x_side, x_cross, x_straight] + list(z_by.values()):
        pl.semaphore_signal(barrier, inc=1, device_id=peer, device_id_type=MESH)

    loads = {}

    def load(key, src, dst):
        copy = pltpu.make_async_copy(src, dst, load_sem.at[len(loads)])
        loads[key] = copy
        return copy

    def load_dec(p, t):
        for m in range(4):
            for r in range(2):
                tile = flip[m] * 8 + (xl if r == 0 else 1 - xl) * 4 + tile_of[p]
                load((p, t, m, r), dec_hbm.at[:, tile, t], dec.at[p, t, m, r])
        when(near_here if t == NEAR else None, lambda: [loads[(p, t, m, r)].start() for m in range(4) for r in range(2)])

    load("ids", ids_hbm.at[0], ids).start()
    for c in range(4):
        part = pl.ds(c * 1024, 1024)
        load(("res", c), res_hbm.at[0, :, part], res.at[:, part]).start()
        load(("enc", c), enc_hbm.at[0, part, :], enc.at[part, :]).start()
    for p in TILES:
        load_dec(p, FAR)
        load_dec(p, NEAR)

    loads["ids"].wait()
    local_ids = ids[...] - feat * 256
    latent = lax.broadcasted_iota(jnp.int32, (256, TOK), 0)
    active = latent == local_ids[0:1, :]
    for k in range(1, 64):
        active = active | (latent == local_ids[k:k + 1, :])
    active = jnp.where(active, 1.0, 0.0).astype(F32).T
    spread = (lax.broadcasted_iota(jnp.int32, (256, 512), 1) // 2 == lax.broadcasted_iota(jnp.int32, (256, 512), 0))
    spread = jnp.where(spread, 1.0, 0.0).astype(BF16)
    pre_acts = jnp.zeros((TOK, 256), F32)
    for c in range(4):
        part = pl.ds(c * 1024, 1024)
        loads[("res", c)].wait()
        loads[("enc", c)].wait()
        pre_acts = pre_acts + jnp.dot(res[:, part], enc[part, :], preferred_element_type=F32)
    acts = (jnp.maximum(pre_acts, 0.0) * active).astype(BF16)
    acts = jnp.dot(acts, spread, preferred_element_type=F32).astype(BF16)
    place = lax.broadcasted_iota(jnp.int32, (TOK, 512), 1) % 2
    for t in range(2):
        for row, low in enumerate((1 - core, core)):
            keep = (place == low) & (2 * t + low >= section)
            lhs[t, pl.ds(row * TOK, TOK), :] = jnp.where(keep, acts, jnp.zeros_like(acts))

    numbers = {}
    pending = []

    def remote(key, src, dst, peer):
        i = numbers.setdefault(key, len(numbers))
        return pltpu.make_async_remote_copy(
            src_ref=src, dst_ref=dst, send_sem=send_sem.at[i], recv_sem=recv_sem.at[i], device_id=peer, device_id_type=MESH
        )

    def send(cond, key, src, dst, peer):
        when(cond, lambda: remote(key, src, dst, peer).start())
        pending.append((cond, key, src, dst, peer))

    def arrived(key, region):
        remote(key, region, region, other_core).wait_recv()

    ALL, BOTH = pl.ds(0, 4), pl.ds(0, 2)

    def out(p, t, m, r, piece):
        return sent.at[p, t, m, r, rows(piece), :]

    def slot(step, p, t, m, r, piece):
        return got.at[step, p, t, m, r, rows(piece), :]

    def have(p, t, m, r, piece):
        return acc[p, t, m, r, rows(piece), :]

    def came(step, p, t, m, r, piece):
        return got[step, p, t, m, r, rows(piece), :].astype(F32)

    def keep(p, t, m, r, piece, value):
        acc[p, t, m, r, rows(piece), :] = value

    def pack(p, t, m, r, piece, value):
        sent[p, t, m, r, rows(piece), :] = value.astype(BF16)

    def multiply(p, far):
        def one(t):
            for m in range(4):
                for r in range(2):
                    loads[(p, t, m, r)].wait()
            for m in range(4):
                w = jnp.concatenate([dec.at[p, t, m, r].reshape(512, 128)[...] for r in range(2)], axis=1)
                both = jnp.dot(lhs[t], w, preferred_element_type=F32)
                for r in range(2):
                    core_out[p, t, m, r] = both[0:TOK, r * 128:(r + 1) * 128].astype(BF16)
                    acc[p, t, m, r] = both[TOK:2 * TOK, r * 128:(r + 1) * 128]

        if far:
            one(FAR)
            send(section != 3, (p, "core", FAR), core_out.at[p, FAR], core_in.at[p, FAR], other_core)
            return
        when(near_here, lambda: one(NEAR))
        send(section == 0, (p, "core", NEAR), core_out.at[p, NEAR], core_in.at[p, NEAR], other_core)

    PATHS = ((1, 1, 3), (3, 2, 1))
    SLOT_OF = ((0, 3), (1, 0))

    def halving(p):
        return p != 0

    def a_rows(p, t, core_sum):
        if not halving(p):
            for m in range(1, 4):
                pack(p, t, m, BOTH, A[t], core_sum(t, m, BOTH, A[t]))
            keep(p, t, 0, BOTH, A[t], core_sum(t, 0, BOTH, A[t]))
            return
        for path, piece in zip(PATHS, SPLIT[t]):
            for m in range(4):
                (pack if m in (path[1], path[1] + 1) else keep)(p, t, m, BOTH, piece, core_sum(t, m, BOTH, piece))

    def a_y_out(p, cond, t):
        if not halving(p):
            for m in (2, 1, 3):
                send(cond, (p, "a y", t, m), out(p, t, m, BOTH, A[t]), slot(0, p, t, m, BOTH, A[t]), y_by[m])
            return
        for path, piece in zip(PATHS, SPLIT[t]):
            send(cond, (p, "a y1", t, path), sent.at[p, t, pl.ds(path[1], 2), BOTH, rows(piece), :],
                 got.at[0, p, t, BOTH, BOTH, rows(piece), :], y_by[path[0]])

    def middle(p):
        def one(t):
            for path, piece, slots in zip(PATHS, SPLIT[t], SLOT_OF):
                k = path[2]
                arrived((p, "a y1", t, path), got.at[0, p, t, BOTH, BOTH, rows(piece), :])
                pack(p, t, k, BOTH, piece, have(p, t, k, BOTH, piece) + came(0, p, t, slots.index(k), BOTH, piece))

        for t, cond in ((FAR, None), (NEAR, near_here)):
            when(cond, lambda: one(t))
            for path, piece in zip(PATHS, SPLIT[t]):
                k = path[2]
                send(cond, (p, "a y2", t, path), out(p, t, k, BOTH, piece), slot(0, p, t, 3, BOTH, piece), y_by[k])

    def a_in(p, t):
        if not halving(p):
            for m in range(1, 4):
                arrived((p, "a y", t, m), slot(0, p, t, m, BOTH, A[t]))
            return
        for path, piece in zip(PATHS, SPLIT[t]):
            arrived((p, "a y2", t, path), slot(0, p, t, 3, BOTH, piece))

    def a_each(p, t, r, put):
        if not halving(p):
            value = have(p, t, 0, r, A[t])
            for m in range(1, 4):
                value = value + came(0, p, t, m, r, A[t])
            put(p, t, 0, r, A[t], value)
            return
        for piece, slots in zip(SPLIT[t], SLOT_OF):
            value = have(p, t, 0, r, piece) + came(0, p, t, slots.index(0), r, piece) + came(0, p, t, 3, r, piece)
            put(p, t, 0, r, piece, value)

    def first(p, far):
        def nothing_came(t):
            core_in[p, t] = jnp.zeros((4, 2, TOK, 128), BF16)

        def core_sum(t, m, r, piece):
            return have(p, t, m, r, piece) + core_in[p, t, m, r, rows(piece), :].astype(F32)

        def b_rows(t):
            for m in range(4):
                pack(p, t, m, 1, B[t], core_sum(t, m, 1, B[t]))
            if t == NEAR:
                for m in range(4):
                    keep(p, t, m, 0, B[t], core_sum(t, m, 0, B[t]))
            else:
                @pl.when(near_here)
                def _():
                    for m in range(4):
                        pack(p, t, m, 0, B[t], core_sum(t, m, 0, B[t]))

                @pl.when(far_here)
                def _():
                    for m in range(4):
                        keep(p, t, m, 0, B[t], core_sum(t, m, 0, B[t]))

        if far:
            when(section != 2, lambda: arrived((p, "core", FAR), core_in.at[p, FAR]))
            when(section == 2, lambda: nothing_came(FAR))
            b_rows(FAR)
            x_out(p, "b", FAR, ALL, B[FAR], (0, 1, 2))
            a_rows(p, FAR, core_sum)
            a_y_out(p, None, FAR)
            return
        when(section == 1, lambda: arrived((p, "core", NEAR), core_in.at[p, NEAR]))
        when(section == 0, lambda: nothing_came(NEAR))
        when(near_here, lambda: b_rows(NEAR))
        x_out(p, "b", NEAR, ALL, B[NEAR], (0, 1, 2))
        when(near_here, lambda: a_rows(p, NEAR, core_sum))
        a_y_out(p, near_here, NEAR)

    def x_out(p, name, t, m, piece, steps):
        side, cross, straight = steps
        if t == NEAR:
            send(near_here, (p, name, "near"), out(p, t, m, 1, piece), slot(side, p, t, m, 0, piece), x_side)
        else:
            send(near_here, (p, name, "straight"), out(p, t, m, 0, piece), slot(straight, p, t, m, 0, piece), x_straight)
            send(near_here, (p, name, "cross"), out(p, t, m, 1, piece), slot(cross, p, t, m, 0, piece), x_cross)
            send(far_here, (p, name, "side"), out(p, t, m, 1, piece), slot(side, p, t, m, 0, piece), x_side)

    def x_in(p, name, t, m, piece, steps):
        side, cross, straight = steps
        if t == NEAR:
            arrived((p, name, "near"), slot(side, p, t, m, 0, piece))
        else:
            arrived((p, name, "side"), slot(side, p, t, m, 0, piece))
            arrived((p, name, "cross"), slot(cross, p, t, m, 0, piece))
            arrived((p, name, "straight"), slot(straight, p, t, m, 0, piece))

    def x_sum(p, t, m, piece, steps):
        value = have(p, t, m, 0, piece)
        for step in steps[:1] if t == NEAR else steps:
            value = value + came(step, p, t, m, 0, piece)
        return value

    def second(p):
        def b_own(t):
            x_in(p, "b", t, ALL, B[t], (0, 1, 2))
            for m in range(1, 4):
                pack(p, t, m, 0, B[t], x_sum(p, t, m, B[t], (0, 1, 2)))
            keep(p, t, 0, 0, B[t], x_sum(p, t, 0, B[t], (0, 1, 2)))

        def a_far():
            a_in(p, FAR)
            a_each(p, FAR, 1, pack)
            when(near_here, lambda: a_each(p, FAR, 0, pack))
            when(far_here, lambda: a_each(p, FAR, 0, keep))

        def a_near():
            a_in(p, NEAR)
            a_each(p, NEAR, 1, pack)
            a_each(p, NEAR, 0, keep)

        def y_out(cond, t):
            for m in (2, 1, 3):
                send(cond, (p, "b y", m), out(p, t, m, 0, B[t]), slot(3, p, t, m, 0, B[t]), y_by[m])

        a_far()
        x_out(p, "a", FAR, 0, A[FAR], (1, 2, 3))
        when(far_here, lambda: b_own(FAR))
        y_out(far_here, FAR)
        when(near_here, lambda: b_own(NEAR))
        y_out(near_here, NEAR)
        when(near_here, a_near)
        x_out(p, "a", NEAR, 0, A[NEAR], (1, 2, 3))

    def third(p):
        def parts(t):
            x_in(p, "a", t, 0, A[t], (1, 2, 3))
            upper = x_sum(p, t, 0, A[t], (1, 2, 3))
            lower = have(p, t, 0, 0, B[t])
            for m in range(1, 4):
                arrived((p, "b y", m), slot(3, p, t, m, 0, B[t]))
                lower = lower + came(3, p, t, m, 0, B[t])
            whole = jnp.concatenate([upper, lower], axis=0).T.reshape(2, 64, TOK)
            z_out[p] = whole.astype(BF16)
            if p == 0:
                z_own[...] = whole

        when(near_here, lambda: parts(NEAR))
        when(far_here, lambda: parts(FAR))
        for e in range(2):
            if (p, e) in z_by:
                send(None, (p, "z", e), z_out.at[p, z_low if e == 0 else 1 - z_low], z_in.at[p, e], z_by[(p, e)])

    pl.semaphore_wait(barrier, 14)
    t0, t1, t2, t3 = TILES
    for stage, *at in (
        (multiply, t0, True), (multiply, t0, False), (multiply, t1, True), (first, t0, True),
        (multiply, t1, False), (first, t0, False), (multiply, t2, True), (first, t1, True),
        (multiply, t2, False), (first, t1, False), (multiply, t3, True), (multiply, t3, False), (middle, t0),
        (first, t2, True), (first, t2, False), (middle, t1), (first, t3, True), (first, t3, False), (middle, t2),
        (second, t0), (second, t1), (second, t2), (third, t0), (second, t3), (third, t1), (third, t2), (third, t3),
    ):
        stage(*at)

    total = z_own[z_low]
    for p in TILES:
        for e in range(2):
            if (p, e) in z_by:
                arrived((p, "z", e), z_in.at[p, e])
                total = total + z_in[p, e].astype(F32)
    out_ref[0] = total.astype(BF16)

    for cond, key, src, dst, peer in pending:
        when(cond, lambda: remote(key, src, dst, peer).wait_send())


def local(residual, enc_weight, dec_weight, latent_ids):
    dec = dec_weight[0].reshape(256, 4, 32, 128).transpose(0, 2, 1, 3).reshape(256, 32, 2, 2, 128)
    ids = latent_ids.transpose(0, 2, 1)
    blocks = (4, 2, 4, 2, TOK, 128)
    return pl.pallas_call(
        kernel,
        out_shape=jax.ShapeDtypeStruct((1, 64, TOK), BF16),
        in_specs=[pl.BlockSpec(memory_space=pl.ANY)] * 4,
        out_specs=pl.BlockSpec(memory_space=pltpu.VMEM),
        scratch_shapes=[
            pltpu.VMEM((TOK, 4096), BF16),
            pltpu.VMEM((4096, 256), BF16),
            pltpu.VMEM((64, TOK), jnp.int32),
            pltpu.VMEM((4, 2, 4, 2, 256, 2, 128), BF16),
            pltpu.VMEM((2, 2 * TOK, 512), BF16),
            pltpu.VMEM(blocks, F32),
            pltpu.VMEM(blocks, BF16),
            pltpu.VMEM(blocks, BF16),
            pltpu.VMEM(blocks, BF16),
            pltpu.VMEM((4,) + blocks, BF16),
            pltpu.VMEM((2, 64, TOK), F32),
            pltpu.VMEM((4, 2, 64, TOK), BF16),
            pltpu.VMEM((4, 2, 64, TOK), BF16),
            pltpu.SemaphoreType.DMA((80,)),
            pltpu.SemaphoreType.DMA((128,)),
            pltpu.SemaphoreType.DMA((128,)),
        ],
        compiler_params=pltpu.CompilerParams(
            collective_id=0, has_side_effects=True, vmem_limit_bytes=60 * 1024 * 1024
        ),
    )(residual, enc_weight, dec, ids)


def solution(mesh):
    in_specs = (
        P("section", None, None),
        P("section", None, "feat"),
        P("section", "feat", None, None),
        P("section", None, None),
    )
    return jax.shard_map(local, mesh=mesh, in_specs=in_specs, out_specs=P("section", "feat", None), check_vma=False)
```
